32 devices in a mesh: fsdp: 4 (over y, x), ctx: 4 (over z), tp: 2 (over core).
Axes of the slice: x: 2, y: 2, z: 4, core: 2. Of those that a mesh axis runs over, the one named last changes fastest.
Arguments:
- tokens: bfloat16 [4, 2048, 1024], P('fsdp', 'ctx'), may hold values from -6 to 6
- segment_ids: int32 [4, 2048], P('fsdp', 'ctx'), may hold values from 0 to 10, as said below
- positions: int32 [4, 2048], P('fsdp', 'ctx'), may hold values from 0 to 2047, as said below
- attention_gain: bfloat16 [1024], P('fsdp'), may hold values from 0.099609375 to 1.8984375
- attention_shift: bfloat16 [1024], P('fsdp'), may hold values from -1.75 to 1.75
- feedforward_gain: bfloat16 [1024], P('fsdp'), may hold values from 0.099609375 to 1.8984375
- feedforward_shift: bfloat16 [1024], P('fsdp'), may hold values from -1.75 to 1.75
- joint_weight: bfloat16 [1024, 3, 1024], P('fsdp', None, 'tp'), may hold values from -8 to 8
- joint_bias: bfloat16 [3, 1024], P(None, ('tp', 'fsdp')), may hold values from -3 to 3
- output_weight: bfloat16 [1024, 1024], P('tp', 'fsdp'), may hold values from -1.5 to 1.5
- output_bias: bfloat16 [1024], P('fsdp'), may hold values from -1.75 to 1.75
- up_weight: bfloat16 [1024, 4096], P('fsdp', 'tp'), may hold values from -0.1875 to 0.1875
- up_bias: bfloat16 [4096], P(('tp', 'fsdp')), may hold values from -3 to 3
- down_weight: bfloat16 [4096, 1024], P('tp', 'fsdp'), may hold values from -0.09375 to 0.09375
- down_bias: bfloat16 [1024], P('fsdp'), may hold values from -1.75 to 1.75
- cotangent: float32 [4, 2048, 1024], P('fsdp', 'ctx'), may hold values from -6 to 6
Outputs:
- result: float32 [4, 2048, 1024], P('fsdp', 'ctx')
- tokens_grad: float32 [4, 2048, 1024], P('fsdp', 'ctx')
- attention_gain_grad: float32 [1024], P('fsdp')
- attention_shift_grad: float32 [1024], P('fsdp')
- feedforward_gain_grad: float32 [1024], P('fsdp')
- feedforward_shift_grad: float32 [1024], P('fsdp')
- joint_weight_grad: float32 [1024, 3, 1024], P('fsdp', None, 'tp')
- joint_bias_grad: float32 [3, 1024], P(None, ('tp', 'fsdp'))
- output_weight_grad: float32 [1024, 1024], P('tp', 'fsdp')
- output_bias_grad: float32 [1024], P('fsdp')
- up_weight_grad: float32 [1024, 4096], P('fsdp', 'tp')
- up_bias_grad: float32 [4096], P(('tp', 'fsdp'))
- down_weight_grad: float32 [4096, 1024], P('tp', 'fsdp')
- down_bias_grad: float32 [1024], P('fsdp')
The draws below stay inside these ranges and needn't reach their ends.
Inputs may be any that keep to these rules, and one draw needn't show every extreme that they name: `segment_ids`: along each sequence the ids start at 0 and rise by one at each document's first token; a document holds 204 to 2048 tokens, the last one cut at the sequence's end. The first sequence is one document; the last sequence is documents of 204 tokens. `positions`: each token's offset from the first token of its document; the first sequence is one document.
All inputs are finite; a program needn't handle non-finite values.
Results may differ from the reference program's by a relative error of at most 0.011.
Values may be sent and summed in bfloat16 or wider, within the bound.
No kernel may reach another device: no remote copies, remote signals or barrier semaphores. Data moves between devices by JAX's collectives and lax.ppermute only.
A program may use at most 192 MiB of HBM per device.

```python
import jax
import jax.numpy as jnp
from jax import lax

D = 1024
H = 16
HD = 64
ROT = 16
FF = 4096
L = 2048
SEQS = 4


def document_layout(key):
    base = jax.random.fold_in(key, 7)
    shortest = max(L // 10, 1)
    lengths = jax.random.randint(base, (SEQS, 16), shortest, L + 1)
    lengths = lengths.at[0].set(L)
    lengths = lengths.at[SEQS - 1].set(shortest)
    ends = jnp.cumsum(lengths, axis=1)
    starts = ends - lengths
    index = jnp.arange(L, dtype=jnp.int32)
    inside = starts[:, None, :] <= index[None, :, None]
    segment = jnp.sum(inside.astype(jnp.int32), axis=2) - 1
    begin = jnp.max(jnp.where(inside, starts[:, None, :], 0), axis=2)
    return (segment.astype(jnp.int32), (index[None, :] - begin).astype(jnp.int32))


def draw_segment_ids(key, part):
    return document_layout(key)[0]


def draw_positions(key, part):
    return document_layout(key)[1]


def draw_joint_weight(key, part):
    matrix = jax.random.normal(key, (D, 3, D), jnp.float32) * D ** (-0.5)
    return jnp.clip(matrix, -8.0, 8.0).astype(jnp.bfloat16)


def shard_levels(key, extent, shards, smallest, largest):
    factor_of, own = 1.0, jax.random.fold_in(key, 6)
    for dim, blocks in shards:
        heights = jnp.exp(jax.random.uniform(jax.random.fold_in(own, dim), (blocks,), jnp.float32, smallest / len(shards), largest / len(shards)))
        factor_of = factor_of * jnp.repeat(heights, extent[dim] // blocks).reshape([-1 if axis == dim else 1 for axis in range(len(extent))])
    return factor_of


def noise(key, extent, deviation, bound, split=(), kind=jnp.bfloat16):
    values = deviation * jax.random.normal(key, extent, jnp.float32)
    if split:
        values = values * shard_levels(key, extent, split, -0.22, 0.18)
    return jnp.clip(values, -bound, bound).astype(kind)


def setup_inputs(seed: int = 0) -> dict:
    splits = jax.random.split(jax.random.key(seed), 17)
    return {
        "tokens": noise(splits[0], (SEQS, L, D), 1.0, 6.0, ((0, 4), (1, 4))),
        "segment_ids": draw_segment_ids(jax.random.fold_in(splits[16], 71), 0),
        "positions": draw_positions(jax.random.fold_in(splits[16], 71), 0),
        "attention_gain": jnp.clip(1.0 + 0.18 * jax.random.normal(splits[3], (D,), jnp.float32), 0.099609375, 1.8984375).astype(jnp.bfloat16),
        "attention_shift": noise(splits[4], (D,), 0.3, 1.75, ((0, 4),)),
        "feedforward_gain": jnp.clip(1.0 + 0.18 * jax.random.normal(splits[5], (D,), jnp.float32), 0.099609375, 1.8984375).astype(jnp.bfloat16),
        "feedforward_shift": noise(splits[6], (D,), 0.3, 1.75, ((0, 4),)),
        "joint_weight": draw_joint_weight(jax.random.fold_in(splits[16], 71), 0),
        "joint_bias": noise(splits[8], (3, D), 0.5, 3.0, ((1, 8),)),
        "output_weight": noise(splits[9], (D, D), 16 ** -0.5, 1.5, ((0, 2), (1, 4))),
        "output_bias": noise(splits[10], (D,), 0.3, 1.75, ((0, 4),)),
        "up_weight": noise(splits[11], (D, FF), D ** -0.5, 0.1875, ((0, 4), (1, 2))),
        "up_bias": noise(splits[12], (FF,), 0.5, 3.0, ((0, 8),)),
        "down_weight": noise(splits[13], (FF, D), FF ** -0.5, 0.09375, ((0, 2), (1, 4))),
        "down_bias": noise(splits[14], (D,), 0.3, 1.75, ((0, 4),)),
        "cotangent": noise(splits[15], (SEQS, L, D), 1.0, 6.0, ((0, 4), (1, 4)), jnp.float32),
    }


EPS = 1e-05
ROPE_BASE = 10000.0

def rope_tables(offsets):
    half_dim = ROT // 2
    freq = ROPE_BASE ** (-(jnp.arange(half_dim, dtype=jnp.float32) * 2.0 / ROT))
    angle = offsets.astype(jnp.float32)[:, None] * freq[None, :]
    return (jnp.cos(angle)[:, None, :], jnp.sin(angle)[:, None, :])

def rotate(tensor, cosine, sine):
    half_dim = ROT // 2
    front = tensor[..., :half_dim]
    middle = tensor[..., half_dim:ROT]
    return jnp.concatenate([front * cosine - middle * sine, middle * cosine + front * sine, tensor[..., ROT:]], axis=-1)

def unrotate(grads, cosine, sine):
    half_dim = ROT // 2
    front = grads[..., :half_dim]
    middle = grads[..., half_dim:ROT]
    return jnp.concatenate([front * cosine + middle * sine, middle * cosine - front * sine, grads[..., ROT:]], axis=-1)

def normalize(rows):
    center = lax.optimization_barrier(jnp.mean(rows, -1, keepdims=True))
    centred = rows - center
    spread = lax.optimization_barrier(jnp.mean(centred * centred, -1, keepdims=True))
    rstd = lax.rsqrt(spread + EPS)
    return (centred * rstd, rstd)

def norm_back(upstream, normed, rstd, gain):
    scaled = upstream * gain
    return rstd * (scaled - lax.optimization_barrier(jnp.mean(scaled, -1, keepdims=True)) - normed * lax.optimization_barrier(jnp.mean(scaled * normed, -1, keepdims=True)))

def masked_scores(query_blk, query_index, query_seg, keys, key_seg):
    scores = jnp.einsum('qhe,khe->hqk', query_blk.astype(jnp.float32), keys.astype(jnp.float32)) * HD ** (-0.5)
    key_index = jnp.arange(keys.shape[0], dtype=jnp.int32)
    allowed = (key_seg[None, :] == query_seg[:, None]) & (key_index[None, :] <= query_index[:, None])
    return jnp.where(allowed[None], scores, -jnp.inf)

def reference(tokens, segment_ids, positions, attention_gain, attention_shift, feedforward_gain, feedforward_shift, joint_weight, joint_bias, output_weight, output_bias, up_weight, up_bias, down_weight, down_bias, cotangent):
    f32 = jnp.float32
    bf16 = jnp.bfloat16
    gain_one = attention_gain.astype(f32)
    shift_one = attention_shift.astype(f32)
    gain_two = feedforward_gain.astype(f32)
    shift_two = feedforward_shift.astype(f32)
    scale = HD ** (-0.5)
    block = min(512, L)
    count_blocks = L // block

    def one_sequence(totals, inputs):
        tok, seg, offs, cot = inputs
        rows = tok.astype(f32)
        normed, rstd = normalize(rows)
        first = (normed * gain_one + shift_one).astype(bf16)
        second = (normed * gain_two + shift_two).astype(bf16)
        joint = jnp.einsum('nd,dpe->npe', first.astype(f32), joint_weight.astype(f32)) + joint_bias.astype(f32)[None]
        cosine, sine = rope_tables(offs)
        queries = rotate(joint[:, 0].reshape(L, H, HD), cosine, sine).astype(bf16)
        keys = rotate(joint[:, 1].reshape(L, H, HD), cosine, sine).astype(bf16)
        values = joint[:, 2].reshape(L, H, HD).astype(bf16)
        index = jnp.arange(L, dtype=jnp.int32)
        query_blocks = queries.reshape(count_blocks, block, H, HD)
        index_blocks = index.reshape(count_blocks, block)
        seg_blocks = seg.reshape(count_blocks, block)

        def forward_block(args):
            query_blk, query_index, query_seg = args
            scores = masked_scores(query_blk, query_index, query_seg, keys, seg)
            top = lax.optimization_barrier(jnp.max(scores, -1, keepdims=True))
            lse = top + jnp.log(lax.optimization_barrier(jnp.sum(jnp.exp(scores - top), -1, keepdims=True)))
            probs = jnp.exp(scores - lse).astype(bf16)
            mixed = jnp.einsum('hqk,khe->qhe', probs.astype(f32), values.astype(f32))
            return (mixed, lse[..., 0])
        context32, lse_all = lax.map(forward_block, (query_blocks, index_blocks, seg_blocks))
        context32 = context32.reshape(L, D)
        context = context32.astype(bf16)
        upper = jnp.dot(second, up_weight, preferred_element_type=f32) + up_bias.astype(f32)
        activated = jax.nn.gelu(upper, approximate=False).astype(bf16)
        result = rows + jnp.dot(context, output_weight, preferred_element_type=f32) + jnp.dot(activated, down_weight, preferred_element_type=f32) + output_bias.astype(f32) + down_bias.astype(f32)
        cot_b = cot.astype(bf16)
        grad_output_w = jnp.dot(context.T, cot_b, preferred_element_type=f32)
        bias_sum = lax.optimization_barrier(jnp.sum(cot, 0))
        grad_down_w = jnp.dot(activated.T, cot_b, preferred_element_type=f32)
        d_act = jnp.dot(cot_b, down_weight.T, preferred_element_type=f32)
        unused, gelu_back = jax.vjp(lambda value: jax.nn.gelu(value, approximate=False), upper)
        d_upper = gelu_back(d_act)[0]
        d_upper_b = d_upper.astype(bf16)
        grad_up_w = jnp.dot(second.T, d_upper_b, preferred_element_type=f32)
        grad_up_b = lax.optimization_barrier(jnp.sum(d_upper, 0))
        d_second = jnp.dot(d_upper_b, up_weight.T, preferred_element_type=f32)
        d_context = jnp.dot(cot_b, output_weight.T, preferred_element_type=f32).astype(bf16).reshape(L, H, HD)
        delta = lax.optimization_barrier(jnp.sum(d_context.astype(f32) * context32.reshape(L, H, HD), -1))

        def backward_block(carry, args):
            query_blk, query_index, query_seg, dctx_blk, delta_blk, lse_blk = args
            scores = masked_scores(query_blk, query_index, query_seg, keys, seg)
            probs = jnp.exp(scores - lse_blk[..., None]).astype(bf16)
            d_probs = jnp.einsum('qhe,khe->hqk', dctx_blk.astype(f32), values.astype(f32))
            d_scores = (probs.astype(f32) * (d_probs - jnp.transpose(delta_blk)[..., None])).astype(bf16)
            d_query_blk = jnp.einsum('hqk,khe->qhe', d_scores.astype(f32), keys.astype(f32)) * scale
            key_add = jnp.einsum('hqk,qhe->khe', d_scores.astype(f32), query_blk.astype(f32)) * scale
            value_add = jnp.einsum('hqk,qhe->khe', probs.astype(f32), dctx_blk.astype(f32))
            return ((carry[0] + key_add, carry[1] + value_add), d_query_blk)
        empty = jnp.zeros((L, H, HD), f32)
        (d_keys, d_values), d_queries = lax.scan(backward_block, (empty, empty), (query_blocks, index_blocks, seg_blocks, d_context.reshape(count_blocks, block, H, HD), delta.reshape(count_blocks, block, H), lse_all))
        d_queries = d_queries.reshape(L, H, HD)
        d_joint = jnp.stack([unrotate(d_queries, cosine, sine).reshape(L, D), unrotate(d_keys, cosine, sine).reshape(L, D), d_values.reshape(L, D)], axis=1)
        d_joint_b = d_joint.astype(bf16)
        grad_joint_w = jnp.einsum('nd,npe->dpe', first.astype(f32), d_joint_b.astype(f32))
        grad_joint_b = lax.optimization_barrier(jnp.sum(d_joint, 0))
        d_first = jnp.einsum('npe,dpe->nd', d_joint_b.astype(f32), joint_weight.astype(f32))
        grads = (lax.optimization_barrier(jnp.sum(d_first * normed, 0)), lax.optimization_barrier(jnp.sum(d_first, 0)), lax.optimization_barrier(jnp.sum(d_second * normed, 0)), lax.optimization_barrier(jnp.sum(d_second, 0)), grad_joint_w, grad_joint_b, grad_output_w, bias_sum, grad_up_w, grad_up_b, grad_down_w, bias_sum)
        tokens_grad = cot + norm_back(d_first, normed, rstd, gain_one) + norm_back(d_second, normed, rstd, gain_two)
        return (tuple((total + grad for total, grad in zip(totals, grads))), (result, tokens_grad))
    start = (jnp.zeros((D,), f32), jnp.zeros((D,), f32), jnp.zeros((D,), f32), jnp.zeros((D,), f32), jnp.zeros((D, 3, D), f32), jnp.zeros((3, D), f32), jnp.zeros((D, D), f32), jnp.zeros((D,), f32), jnp.zeros((D, FF), f32), jnp.zeros((FF,), f32), jnp.zeros((FF, D), f32), jnp.zeros((D,), f32))
    totals, outputs = lax.scan(one_sequence, start, (tokens, segment_ids, positions, cotangent))
    result, tokens_grad = outputs
    return (result, tokens_grad, totals[0], totals[1], totals[2], totals[3], totals[4], totals[5], totals[6], totals[7], totals[8], totals[9], totals[10], totals[11])
```

```python
import jax
import jax.numpy as jnp
from jax import lax
from jax.experimental import pallas as pl
from jax.experimental.pallas import tpu as pltpu
from jax.sharding import PartitionSpec as P

HD = 64
ROT = 16


EPS = 1e-05
ROPE_BASE = 10000.0


def rope_tables(offsets):
    half_dim = ROT // 2
    freq = ROPE_BASE ** (-(jnp.arange(half_dim, dtype=jnp.float32) * 2.0 / ROT))
    angle = offsets.astype(jnp.float32)[:, None] * freq[None, :]
    return (jnp.cos(angle)[:, None, :], jnp.sin(angle)[:, None, :])


def rotate(tensor, cosine, sine):
    half_dim = ROT // 2
    front = tensor[..., :half_dim]
    middle = tensor[..., half_dim:ROT]
    return jnp.concatenate(
        [front * cosine - middle * sine, middle * cosine + front * sine, tensor[..., ROT:]], axis=-1
    )


def unrotate(grads, cosine, sine):
    half_dim = ROT // 2
    front = grads[..., :half_dim]
    middle = grads[..., half_dim:ROT]
    return jnp.concatenate(
        [front * cosine + middle * sine, middle * cosine - front * sine, grads[..., ROT:]], axis=-1
    )


def normalize(rows):
    center = jnp.mean(rows, -1, keepdims=True)
    centred = rows - center
    spread = jnp.mean(centred * centred, -1, keepdims=True)
    rstd = lax.rsqrt(spread + EPS)
    return (centred * rstd, rstd)


def norm_back(upstream, normed, rstd, gain):
    scaled = upstream * gain
    return rstd * (
        scaled
        - jnp.mean(scaled, -1, keepdims=True)
        - normed * jnp.mean(scaled * normed, -1, keepdims=True)
    )


def masked_scores(query_blk, query_index, query_seg, keys, key_seg):
    scores = jnp.einsum(
        "qhe,khe->hqk", query_blk, keys, preferred_element_type=jnp.float32
    ) * HD ** (-0.5)
    key_index = jnp.arange(keys.shape[0], dtype=jnp.int32)
    allowed = (key_seg[None, :] == query_seg[:, None]) & (
        key_index[None, :] <= query_index[:, None]
    )
    return jnp.where(allowed[None], scores, -jnp.inf)


def gathered_local(
    tokens,
    segment_ids,
    positions,
    attention_gain,
    attention_shift,
    feedforward_gain,
    feedforward_shift,
    joint_weight,
    joint_bias,
    output_weight,
    output_bias,
    up_weight,
    up_bias,
    down_weight,
    down_bias,
    cotangent,
):
    f32 = jnp.float32
    bf16 = jnp.bfloat16
    scale = HD ** (-0.5)
    small = jnp.stack(
        [
            attention_gain,
            attention_shift,
            feedforward_gain,
            feedforward_shift,
            output_bias,
            down_bias,
        ]
    )
    full_joint, full_output, full_up, full_down, full_small, full_jbias, full_upbias = (
        lax.all_gather(joint_weight, "fsdp", axis=0, tiled=True),
        lax.all_gather(output_weight, "fsdp", axis=1, tiled=True),
        lax.all_gather(up_weight, "fsdp", axis=0, tiled=True),
        lax.all_gather(down_weight, "fsdp", axis=1, tiled=True),
        lax.all_gather(small, "fsdp", axis=1, tiled=True),
        lax.all_gather(joint_bias, "fsdp", axis=1, tiled=True),
        lax.all_gather(up_bias, "fsdp", axis=0, tiled=True),
    )
    params = full_small.astype(f32)
    gain_one = params[0]
    shift_one = params[1]
    gain_two = params[2]
    shift_two = params[3]
    rows = tokens[0].astype(f32)
    count_rows = rows.shape[0]
    local_width = joint_weight.shape[2]
    heads_here = local_width // HD
    normed, rstd = normalize(rows)
    first = (normed * gain_one + shift_one).astype(bf16)
    second = (normed * gain_two + shift_two).astype(bf16)
    joint = (
        jnp.einsum("nd,dpe->npe", first, full_joint, preferred_element_type=f32)
        + full_jbias.astype(f32)[None]
    )
    cosine, sine = rope_tables(positions[0])
    queries = rotate(joint[:, 0].reshape(count_rows, heads_here, HD), cosine, sine).astype(bf16)
    keys_here = rotate(joint[:, 1].reshape(count_rows, heads_here, HD), cosine, sine).astype(bf16)
    values_here = joint[:, 2].reshape(count_rows, heads_here, HD).astype(bf16)
    seg_here = segment_ids[0]
    all_keys, all_values, all_segs = (
        lax.all_gather(keys_here, "ctx", axis=0, tiled=True),
        lax.all_gather(values_here, "ctx", axis=0, tiled=True),
        lax.all_gather(seg_here.astype(bf16), "ctx", axis=0, tiled=True),
    )
    key_seg = all_segs.astype(f32)
    query_seg = seg_here.astype(f32)
    query_index = lax.axis_index("ctx") * count_rows + jnp.arange(count_rows, dtype=jnp.int32)
    block = min(512, count_rows)
    count_blocks = count_rows // block
    query_blocks = queries.reshape(count_blocks, block, heads_here, HD)
    index_blocks = query_index.reshape(count_blocks, block)
    seg_blocks = query_seg.reshape(count_blocks, block)

    def forward_block(args):
        query_blk, block_index, block_seg = args
        scores = masked_scores(query_blk, block_index, block_seg, all_keys, key_seg)
        top = jnp.max(scores, -1, keepdims=True)
        lse = top + jnp.log(jnp.sum(jnp.exp(scores - top), -1, keepdims=True))
        probs = jnp.exp(scores - lse).astype(bf16)
        mixed = jnp.einsum("hqk,khe->qhe", probs, all_values, preferred_element_type=f32)
        return (mixed, lse[..., 0])

    context32, lse_all = lax.map(forward_block, (query_blocks, index_blocks, seg_blocks))
    context32 = context32.reshape(count_rows, local_width)
    context = context32.astype(bf16)
    upper = jnp.dot(second, full_up, preferred_element_type=f32) + full_upbias.astype(f32)
    activated = jax.nn.gelu(upper, approximate=False).astype(bf16)
    partial_value = jnp.dot(context, full_output, preferred_element_type=f32) + jnp.dot(
        activated, full_down, preferred_element_type=f32
    )
    mixed_all = lax.psum(partial_value, "tp")
    result = rows + mixed_all + params[4] + params[5]
    back_joint, back_output, back_up, back_down = (
        lax.all_gather(joint_weight, "fsdp", axis=0, tiled=True),
        lax.all_gather(output_weight, "fsdp", axis=1, tiled=True),
        lax.all_gather(up_weight, "fsdp", axis=0, tiled=True),
        lax.all_gather(down_weight, "fsdp", axis=1, tiled=True),
    )
    cot = cotangent[0]
    cot_b = cot.astype(bf16)
    grad_output_w = jnp.dot(context.T, cot_b, preferred_element_type=f32)
    bias_sum = jnp.sum(cot, 0)
    grad_down_w = jnp.dot(activated.T, cot_b, preferred_element_type=f32)
    d_act = jnp.einsum("nd,fd->nf", cot_b, back_down, preferred_element_type=f32)
    unused, gelu_back = jax.vjp(lambda value: jax.nn.gelu(value, approximate=False), upper)
    d_upper = gelu_back(d_act)[0]
    d_upper_b = d_upper.astype(bf16)
    grad_up_w = jnp.dot(second.T, d_upper_b, preferred_element_type=f32)
    grad_up_b = jnp.sum(d_upper, 0)
    d_second_part = jnp.einsum("nf,df->nd", d_upper_b, back_up, preferred_element_type=f32)
    d_context = (
        jnp.einsum("nd,wd->nw", cot_b, back_output, preferred_element_type=f32)
        .astype(bf16)
        .reshape(count_rows, heads_here, HD)
    )
    delta = jnp.sum(d_context.astype(f32) * context32.reshape(count_rows, heads_here, HD), -1)
    dctx_blocks = d_context.reshape(count_blocks, block, heads_here, HD)

    def backward_block(args):
        query_blk, block_index, block_seg, dctx_blk, delta_blk, lse_blk = args
        scores = masked_scores(query_blk, block_index, block_seg, all_keys, key_seg)
        probs = jnp.exp(scores - lse_blk[..., None]).astype(bf16)
        d_probs = jnp.einsum("qhe,khe->hqk", dctx_blk, all_values, preferred_element_type=f32)
        d_scores = (probs.astype(f32) * (d_probs - jnp.transpose(delta_blk)[..., None])).astype(
            bf16
        )
        d_query_blk = (
            jnp.einsum("hqk,khe->qhe", d_scores, all_keys, preferred_element_type=f32) * scale
        )
        return (probs, d_scores, d_query_blk)

    probs_all, dscores_all, d_queries = lax.map(
        backward_block,
        (
            query_blocks,
            index_blocks,
            seg_blocks,
            dctx_blocks,
            delta.reshape(count_blocks, block, heads_here),
            lse_all,
        ),
    )
    d_queries = d_queries.reshape(count_rows, heads_here, HD)
    key_part = (
        jnp.einsum("bhqk,bqhe->khe", dscores_all, query_blocks, preferred_element_type=f32) * scale
    )
    value_part = jnp.einsum("bhqk,bqhe->khe", probs_all, dctx_blocks, preferred_element_type=f32)
    key_value = lax.psum_scatter(
        jnp.concatenate(
            [
                key_part.reshape(count_rows * lax.axis_size("ctx"), local_width),
                value_part.reshape(count_rows * lax.axis_size("ctx"), local_width),
            ],
            axis=1,
        ),
        "ctx",
        scatter_dimension=0,
        tiled=True,
    )
    d_keys = key_value[:, :local_width].reshape(count_rows, heads_here, HD)
    d_values = key_value[:, local_width:]
    d_joint = jnp.stack(
        [
            unrotate(d_queries, cosine, sine).reshape(count_rows, local_width),
            unrotate(d_keys, cosine, sine).reshape(count_rows, local_width),
            d_values,
        ],
        axis=1,
    )
    d_joint_b = d_joint.astype(bf16)
    grad_joint_w = jnp.einsum("nd,npe->dpe", first, d_joint_b, preferred_element_type=f32)
    grad_joint_b = jnp.sum(d_joint, 0)
    d_first_part = jnp.einsum("npe,dpe->nd", d_joint_b, back_joint, preferred_element_type=f32)
    d_first, d_second = lax.psum((d_first_part, d_second_part), "tp")
    norm_stats = jnp.stack(
        [
            jnp.sum(d_first * normed, 0),
            jnp.sum(d_first, 0),
            jnp.sum(d_second * normed, 0),
            jnp.sum(d_second, 0),
        ]
    )
    tokens_grad = (
        cot
        + norm_back(d_first, normed, rstd, gain_one)
        + norm_back(d_second, normed, rstd, gain_two)
    )
    grad_small = jnp.concatenate([norm_stats, bias_sum[None], bias_sum[None]], axis=0)
    share_joint, share_output, share_up, share_down, share_small, share_jbias, share_upbias = (
        lax.psum_scatter(grad_joint_w, ("fsdp", "ctx"), scatter_dimension=0, tiled=True),
        lax.psum_scatter(grad_output_w, ("fsdp", "ctx"), scatter_dimension=1, tiled=True),
        lax.psum_scatter(grad_up_w, ("fsdp", "ctx"), scatter_dimension=0, tiled=True),
        lax.psum_scatter(grad_down_w, ("fsdp", "ctx"), scatter_dimension=1, tiled=True),
        lax.psum_scatter(grad_small, ("fsdp", "ctx"), scatter_dimension=1, tiled=True),
        lax.psum_scatter(grad_joint_b, ("fsdp", "ctx"), scatter_dimension=1, tiled=True),
        lax.psum_scatter(grad_up_b, ("fsdp", "ctx"), scatter_dimension=0, tiled=True),
    )
    owned = (
        lax.all_gather(share_joint, "ctx", axis=0, tiled=True),
        lax.all_gather(share_output, "ctx", axis=1, tiled=True),
        lax.all_gather(share_up, "ctx", axis=0, tiled=True),
        lax.all_gather(share_down, "ctx", axis=1, tiled=True),
        lax.all_gather(share_small, "ctx", axis=1, tiled=True),
        lax.all_gather(share_jbias, "ctx", axis=1, tiled=True),
        lax.all_gather(share_upbias, "ctx", axis=0, tiled=True),
    )
    owned_joint, owned_output, owned_up, owned_down, owned_small, owned_jbias, owned_upbias = owned
    return (
        result[None],
        tokens_grad[None],
        owned_small[0],
        owned_small[1],
        owned_small[2],
        owned_small[3],
        owned_joint,
        owned_jbias,
        owned_output,
        owned_small[4],
        owned_up,
        owned_upbias,
        owned_down,
        owned_small[5],
    )


NEG = -1e30


def attention_body(
    heads, q_ref, k_ref, v_ref, dc_ref, qseg_ref, kseg_ref, ctx_ref, dq_ref, dkv_ref,
    kt_ref, vt_ref, s_ref, e_ref, dk_acc, dv_acc,
):
    f32 = jnp.float32
    bf16 = jnp.bfloat16
    step = pl.program_id(0)
    rows, width = q_ref.shape
    chunks, _, chunk = kt_ref.shape
    hd = width // heads

    @pl.when(step == 0)
    def _():
        for c in range(chunks):
            part = pl.ds(c * chunk, chunk)
            kt_ref[c] = k_ref[part, :].astype(f32).T.astype(bf16)
            vt_ref[c] = v_ref[part, :].astype(f32).T.astype(bf16)
        dk_acc[...] = jnp.zeros_like(dk_acc)
        dv_acc[...] = jnp.zeros_like(dv_acc)

    used = ((step + 1) * rows + chunk - 1) // chunk
    q = q_ref[...]
    q_t = q.astype(f32).T
    dc_t = dc_ref[...].astype(f32).T
    row_head = lax.broadcasted_iota(jnp.int32, (width, rows), 0) // hd
    lane_head = lax.broadcasted_iota(jnp.int32, (rows, width), 1) // hd
    q_heads_t = [jnp.where(row_head == h, q_t, 0.0).astype(bf16) for h in range(heads)]
    q_heads = [jnp.where(lane_head == h, q, jnp.zeros_like(q)) for h in range(heads)]
    qseg = qseg_ref[...]
    query = step * rows + lax.broadcasted_iota(jnp.int32, (1, rows), 1)
    key_base = lax.broadcasted_iota(jnp.int32, (chunk, 1), 0)

    def score(j, tops):
        part = pl.ds(pl.multiple_of(j * chunk, chunk), chunk)
        keys = k_ref[part, :]
        allowed = (kseg_ref[part, :] == qseg) & (key_base + j * chunk <= query)
        out = []
        for h in range(heads):
            s = jnp.dot(keys, q_heads_t[h], preferred_element_type=f32)
            s = jnp.where(allowed, s, NEG)
            s_ref[h, part, :] = s
            out.append(jnp.maximum(tops[h], jnp.max(s, 0, keepdims=True)))
        return tuple(out)

    tops = lax.fori_loop(
        0, used, score, tuple(jnp.full((1, rows), NEG, f32) for _ in range(heads))
    )

    def mix(j, carry):
        part = pl.ds(pl.multiple_of(j * chunk, chunk), chunk)
        values_t = vt_ref[j]
        out = []
        for h in range(heads):
            total, acc = carry[h]
            e = jnp.exp(s_ref[h, part, :] - tops[h])
            total = total + jnp.sum(e, 0, keepdims=True)
            e = e.astype(bf16)
            e_ref[h, part, :] = e
            acc = acc + jnp.dot(
                values_t[h * hd : (h + 1) * hd, :], e, preferred_element_type=f32
            )
            out.append((total, acc))
        return tuple(out)

    mixed = lax.fori_loop(
        0,
        used,
        mix,
        tuple((jnp.zeros((1, rows), f32), jnp.zeros((hd, rows), f32)) for _ in range(heads)),
    )
    ctx_parts, dcn_parts, deltas = [], [], []
    for h in range(heads):
        total, acc = mixed[h]
        inv = 1.0 / total
        ctx_h = acc * inv
        dc_h = dc_t[h * hd : (h + 1) * hd, :]
        deltas.append(jnp.sum(ctx_h * dc_h, 0, keepdims=True) * inv)
        ctx_parts.append(ctx_h)
        dcn_parts.append(dc_h * inv)
    ctx_ref[...] = jnp.concatenate(ctx_parts, 0).T.astype(bf16)
    dcn_t = jnp.concatenate(dcn_parts, 0)
    dcn = dcn_t.T
    dcn_heads_t = [jnp.where(row_head == h, dcn_t, 0.0).astype(bf16) for h in range(heads)]
    dcn_heads = [jnp.where(lane_head == h, dcn, 0.0).astype(bf16) for h in range(heads)]

    def back(j, carry):
        part = pl.ds(pl.multiple_of(j * chunk, chunk), chunk)
        values = v_ref[part, :]
        keys_t = kt_ref[j]
        dk = dk_acc[part, :]
        dv = dv_acc[part, :]
        out = []
        for h in range(heads):
            e = e_ref[h, part, :]
            dp = jnp.dot(values, dcn_heads_t[h], preferred_element_type=f32)
            ds = (e.astype(f32) * (dp - deltas[h])).astype(bf16)
            out.append(
                carry[h]
                + jnp.dot(keys_t[h * hd : (h + 1) * hd, :], ds, preferred_element_type=f32)
            )
            dk = dk + jnp.dot(ds, q_heads[h], preferred_element_type=f32)
            dv = dv + jnp.dot(e, dcn_heads[h], preferred_element_type=f32)
        dk_acc[part, :] = dk
        dv_acc[part, :] = dv
        return tuple(out)

    dq = lax.fori_loop(
        0, used, back, tuple(jnp.zeros((hd, rows), f32) for _ in range(heads))
    )
    dq_ref[...] = (jnp.concatenate(dq, 0).T * HD ** (-0.5)).astype(bf16)

    @pl.when(step == pl.num_programs(0) - 1)
    def _():
        dkv_ref[:, :width] = dk_acc[...].astype(bf16)
        dkv_ref[:, width:] = dv_acc[...].astype(bf16)


def attention(qkv, dctx, seg, block=256, chunk=256):
    count, width = dctx.shape
    heads = width // HD
    bf16 = jnp.bfloat16
    f32 = jnp.float32
    pairs = count * (count + block) // 2 * heads
    return pl.pallas_call(
        lambda *refs: attention_body(heads, *refs),
        grid=(count // block,),
        in_specs=[
            pl.BlockSpec((block, width), lambda i: (i, 0)),
            pl.BlockSpec((count, width), lambda i: (0, 1)),
            pl.BlockSpec((count, width), lambda i: (0, 2)),
            pl.BlockSpec((block, width), lambda i: (i, 0)),
            pl.BlockSpec((1, block), lambda i: (0, i)),
            pl.BlockSpec((count, 1), lambda i: (0, 0)),
        ],
        out_specs=[
            pl.BlockSpec((block, width), lambda i: (i, 0)),
            pl.BlockSpec((block, width), lambda i: (i, 0)),
            pl.BlockSpec((count, 2 * width), lambda i: (0, 0)),
        ],
        out_shape=[
            jax.ShapeDtypeStruct((count, width), bf16),
            jax.ShapeDtypeStruct((count, width), bf16),
            jax.ShapeDtypeStruct((count, 2 * width), bf16),
        ],
        scratch_shapes=[
            pltpu.VMEM((count // chunk, width, chunk), bf16),
            pltpu.VMEM((count // chunk, width, chunk), bf16),
            pltpu.VMEM((heads, count, block), f32),
            pltpu.VMEM((heads, count, block), bf16),
            pltpu.VMEM((count, width), f32),
            pltpu.VMEM((count, width), f32),
        ],
        compiler_params=pltpu.CompilerParams(vmem_limit_bytes=40 * 1024 * 1024),
        cost_estimate=pl.CostEstimate(
            flops=10 * pairs * HD * 3, bytes_accessed=count * width * 16, transcendentals=pairs
        ),
        name="attention",
    )(qkv, qkv, qkv, dctx, seg[None, :], seg[:, None])


def partner(tensor, axis, flip):
    size = lax.axis_size(axis)
    return lax.ppermute(tensor, axis, [(s, s ^ flip) for s in range(size)])


def pick(tensor, index, size, dim=0):
    return lax.dynamic_slice_in_dim(tensor, index * size, size, dim)


def put(buffer, block, index, dim=0):
    return lax.dynamic_update_slice_in_dim(buffer, block, index * block.shape[dim], dim)


def exchange(tensor, axis, dim_from, dim_to):
    size = lax.axis_size(axis)
    me = lax.axis_index(axis)
    part = tensor.shape[dim_from] // size
    shape = list(tensor.shape)
    shape[dim_from] = part
    shape[dim_to] *= size
    out = jnp.zeros(shape, tensor.dtype)
    for flip in range(size):
        block = pick(tensor, me ^ flip, part, dim_from)
        if flip:
            block = partner(block, axis, flip)
        out = put(out, block, me ^ flip, dim_to)
    return out


def plane_gather(block, axis="fsdp"):
    return [block] + [partner(block, axis, flip) for flip in range(1, lax.axis_size(axis))]


def chip_gather(rows):
    core = lax.axis_index("tp")
    half = rows.shape[0] // 2
    mine = pick(rows, core, half)
    out = [rows]
    for block in plane_gather(mine)[1:]:
        other = partner(block, "tp", 1)
        out.append(jnp.where(core == 0, block, other))
        out.append(jnp.where(core == 0, other, block))
    return jnp.concatenate(out, 0)


def chip_scatter(partial, count):
    f32 = jnp.float32
    bf16 = jnp.bfloat16
    core = lax.axis_index("tp")
    size = partial.shape[0] // count
    halves = partial.reshape(size, 2, count // 2, partial.shape[1])
    away = lax.dynamic_index_in_dim(halves, 1 - core, 1, keepdims=False).astype(bf16)
    kept = lax.dynamic_index_in_dim(halves, core, 1, keepdims=False)
    summed = kept + partner(away, "tp", 1).astype(f32)
    sending = summed.astype(bf16)
    total = summed[0]
    for flip in range(1, size):
        total = total + partner(sending[flip], "fsdp", flip).astype(f32)
    other = partner(total, "tp", 1)
    low = jnp.where(core == 0, total, other)
    high = jnp.where(core == 0, other, total)
    return jnp.concatenate([low, high], 0)


def spread_sum(parts, axis):
    size = lax.axis_size(axis)
    me = lax.axis_index(axis)
    total = lax.dynamic_index_in_dim(parts, me, 1, keepdims=False).astype(jnp.float32)
    for flip in range(1, size):
        block = lax.dynamic_index_in_dim(parts, me ^ flip, 1, keepdims=False)
        total = total + partner(block, axis, flip).astype(jnp.float32)
    return total


def share_rows(grad):
    size, depth = lax.axis_size("fsdp"), lax.axis_size("ctx")
    rows, cols = grad.shape
    part = rows // size // depth
    quarter = spread_sum(grad.reshape(size, depth, part, cols), "ctx").astype(jnp.bfloat16)
    me, place = lax.axis_index("fsdp"), lax.axis_index("ctx")
    held = jnp.zeros((part, size, cols), jnp.bfloat16)
    for flip in range(size):
        block = lax.dynamic_index_in_dim(quarter, me ^ flip, 0, keepdims=False)
        if flip:
            block = partner(block, "fsdp", flip)
        held = lax.dynamic_update_slice(held, block[:, None], (0, me ^ flip, 0))
    out = jnp.zeros((depth, part, size, cols), jnp.float32)
    for flip in range(depth):
        block = partner(held, "ctx", flip) if flip else held
        out = lax.dynamic_update_slice(
            out, block.astype(jnp.float32)[None], (place ^ flip, 0, 0, 0)
        )
    return out.reshape(rows // size, size, cols)


def share_cols(grad):
    size, depth = lax.axis_size("fsdp"), lax.axis_size("ctx")
    rows, cols = grad.shape
    part = rows // depth
    width = cols // size
    quarter = spread_sum(grad.reshape(1, depth, part, cols), "ctx")[0].astype(jnp.bfloat16)
    me, place = lax.axis_index("fsdp"), lax.axis_index("ctx")
    held = jnp.zeros((size, part, width), jnp.bfloat16)
    for flip in range(size):
        block = pick(quarter, me ^ flip, width, 1)
        if flip:
            block = partner(block, "fsdp", flip)
        held = lax.dynamic_update_slice(held, block[None], (me ^ flip, 0, 0))
    out = jnp.zeros((size, depth, part, width), jnp.float32)
    for flip in range(depth):
        block = partner(held, "ctx", flip) if flip else held
        out = lax.dynamic_update_slice(
            out, block.astype(jnp.float32)[:, None], (0, place ^ flip, 0, 0)
        )
    return out.reshape(size * rows, width)


def all_sum(vector, axis):
    total = vector
    for flip in range(1, lax.axis_size(axis)):
        total = total + partner(vector, axis, flip)
    return total


def plane_local(
    tokens,
    segment_ids,
    positions,
    attention_gain,
    attention_shift,
    feedforward_gain,
    feedforward_shift,
    joint_weight,
    joint_bias,
    output_weight,
    output_bias,
    up_weight,
    up_bias,
    down_weight,
    down_bias,
    cotangent,
):
    f32 = jnp.float32
    bf16 = jnp.bfloat16
    me, place, core = lax.axis_index("fsdp"), lax.axis_index("ctx"), lax.axis_index("tp")
    size = lax.axis_size("fsdp")
    count, model = tokens.shape[1:]
    rows = tokens[0].astype(f32)
    cot = cotangent[0]

    small = jnp.concatenate(
        [
            attention_gain,
            attention_shift,
            feedforward_gain,
            feedforward_shift,
            output_bias,
            down_bias,
        ]
    ).reshape(6, -1)
    full_small = jnp.zeros((6, model), bf16)
    for flip, block in enumerate(plane_gather(small)):
        full_small = put(full_small, block, me ^ flip, 1)
    params = full_small.astype(f32)
    ids = jnp.concatenate([segment_ids, positions], 0)
    ids_plane = plane_gather(ids)
    pos_plane = jnp.concatenate([block[1] for block in ids_plane])
    seg_plane = jnp.concatenate([block[0] for block in ids_plane])

    plane_tokens = chip_gather(tokens[0])
    width = joint_weight.shape[2] // size
    joint_w = exchange(joint_weight, "fsdp", 2, 0)
    cot_b = chip_gather(cot.astype(bf16))
    output_w = exchange(output_weight, "fsdp", 0, 1)
    up_w = exchange(up_weight, "fsdp", 1, 0)
    down_w = exchange(down_weight, "fsdp", 0, 1)

    normed, _ = normalize(plane_tokens.astype(f32))
    first = (normed * params[0] + params[1]).astype(bf16)
    second = (normed * params[2] + params[3]).astype(bf16)

    lane = jnp.arange(width, dtype=jnp.int32) % HD
    half = ROT // 2
    freq = jnp.where(
        lane < ROT, ROPE_BASE ** (-((lane % half).astype(f32) * 2.0 / ROT)), 0.0
    )
    angle = pos_plane.astype(f32)[:, None] * freq[None, :]
    cosine = jnp.cos(angle)
    sine = jnp.sin(angle) * jnp.where(lane < half, -1.0, 1.0)[None, :]
    source = jnp.arange(width, dtype=jnp.int32)
    source = jnp.where(lane < half, source + half, jnp.where(lane < ROT, source - half, -1))
    swap = (jnp.arange(width, dtype=jnp.int32)[:, None] == source[None, :]).astype(bf16)

    joint_flat = joint_w.reshape(model, 3 * width)
    bias = joint_bias.astype(f32)
    joint = jnp.dot(first, joint_flat, preferred_element_type=f32) + bias.reshape(-1)[None]
    swapped_w = jnp.einsum("dpe,ef->dpf", joint_w[:, :2], swap, preferred_element_type=bf16)
    swapped_b = jnp.dot(joint_bias[:2], swap, preferred_element_type=f32)
    swapped = (
        jnp.dot(first, swapped_w.reshape(model, 2 * width), preferred_element_type=f32)
        + swapped_b.reshape(-1)[None]
    )
    scale = HD ** (-0.5)
    queries = (joint[:, :width] * cosine + swapped[:, :width] * sine) * scale
    keys = joint[:, width : 2 * width] * cosine + swapped[:, width:] * sine
    qkv = jnp.concatenate([queries, keys, joint[:, 2 * width :]], 1).astype(bf16)

    def to_sequence(tensor):
        out = jnp.zeros(tensor.shape, tensor.dtype)
        for flip in range(size):
            block = pick(tensor, me ^ place ^ flip, count)
            if flip:
                block = partner(block, "ctx", flip)
            out = put(out, block, place ^ flip)
        return out

    def from_sequence(tensor):
        out = jnp.zeros(tensor.shape, tensor.dtype)
        for flip in range(size):
            block = pick(tensor, place ^ flip, count)
            if flip:
                block = partner(block, "ctx", flip)
            out = put(out, block, me ^ place ^ flip)
        return out

    seg_seq = to_sequence(seg_plane)
    qkv_seq = to_sequence(qkv)
    d_context = jnp.einsum("nd,wd->nw", cot_b, output_w, preferred_element_type=f32).astype(bf16)
    dctx_seq = to_sequence(d_context)
    ctx_seq, dq_seq, dkv_seq = attention(qkv_seq, dctx_seq, seg_seq)

    upper = jnp.dot(second, up_w, preferred_element_type=f32) + up_bias.astype(f32)[None]
    gelu, gelu_back = jax.vjp(lambda value: jax.nn.gelu(value, approximate=False), upper)
    activated = gelu.astype(bf16)
    d_act = jnp.einsum("nd,fd->nf", cot_b, down_w, preferred_element_type=f32)
    d_upper = gelu_back(d_act)[0]
    d_upper_b = d_upper.astype(bf16)
    grad_up_b = jnp.sum(d_upper, 0)
    grad_up_w = jnp.dot(second.T, d_upper_b, preferred_element_type=f32).astype(bf16)
    grad_down_w = jnp.dot(activated.T, cot_b, preferred_element_type=f32).astype(bf16)
    d_second = jnp.einsum("nf,df->nd", d_upper_b, up_w, preferred_element_type=f32)

    context = from_sequence(ctx_seq)
    mixed = jnp.dot(context, output_w, preferred_element_type=f32) + jnp.dot(
        activated, down_w, preferred_element_type=f32
    )
    result = rows + chip_scatter(mixed, count) + params[4] + params[5]
    grad_output_w = jnp.dot(context.T, cot_b, preferred_element_type=f32).astype(bf16)

    dq = from_sequence(dq_seq)
    dkv = from_sequence(dkv_seq)
    dq_swapped = jnp.dot(dq, swap, preferred_element_type=f32)
    dk_swapped = jnp.dot(dkv[:, :width], swap, preferred_element_type=f32)
    d_joint = jnp.concatenate(
        [
            dq.astype(f32) * cosine - dq_swapped * sine,
            dkv[:, :width].astype(f32) * cosine - dk_swapped * sine,
            dkv[:, width:].astype(f32),
        ],
        1,
    )
    d_joint_b = d_joint.astype(bf16)
    grad_joint_b = jnp.sum(d_joint, 0)
    grad_joint_w = jnp.dot(first.T, d_joint_b, preferred_element_type=f32).astype(bf16)
    d_first = jnp.einsum("ne,de->nd", d_joint_b, joint_flat, preferred_element_type=f32)
    upstream = chip_scatter(d_first * params[0] + d_second * params[2], count)

    normed_here, rstd = normalize(rows)
    tokens_grad = cot + rstd * (
        upstream
        - jnp.mean(upstream, -1, keepdims=True)
        - normed_here * jnp.mean(upstream * normed_here, -1, keepdims=True)
    )
    stats = jnp.stack(
        [
            jnp.sum(d_first * normed, 0),
            jnp.sum(d_first, 0),
            jnp.sum(d_second * normed, 0),
            jnp.sum(d_second, 0),
            jnp.sum(pick(cot, core, count // 2), 0),
        ]
    )
    stats = spread_sum(stats.reshape(5, size, -1), "fsdp")
    stats = all_sum(stats, "tp")
    packed = jnp.concatenate([stats.reshape(-1), grad_joint_b, grad_up_b])
    packed = all_sum(packed, "ctx")
    owned = packed[: stats.size].reshape(stats.shape)
    owned_jbias = packed[stats.size : stats.size + 3 * width].reshape(3, width)
    owned_upbias = packed[stats.size + 3 * width :]

    owned_up = share_rows(grad_up_w).reshape(up_weight.shape)
    owned_down = share_cols(grad_down_w)
    owned_output = share_cols(grad_output_w)
    owned_joint = share_rows(grad_joint_w).reshape(model // size, size, 3, width)
    owned_joint = owned_joint.transpose(0, 2, 1, 3).reshape(joint_weight.shape)
    return (
        result[None],
        tokens_grad[None],
        owned[0],
        owned[1],
        owned[2],
        owned[3],
        owned_joint,
        owned_jbias,
        owned_output,
        owned[4],
        owned_up,
        owned_upbias,
        owned_down,
        owned[4],
    )


def splits_plane(mesh, tokens, joint_weight):
    size, depth, cores = mesh.shape["fsdp"], mesh.shape["ctx"], mesh.shape["tp"]
    width = joint_weight.shape[2] // (size * cores)
    return (
        size == depth == tokens.shape[0]
        and size & (size - 1) == 0
        and cores == 2
        and width % 128 == 0
        and tokens.shape[1] // depth % 256 == 0
    )


def solution(mesh):
    placed = (
        P("fsdp", "ctx", None),
        P("fsdp", "ctx"),
        P("fsdp", "ctx"),
        P("fsdp"),
        P("fsdp"),
        P("fsdp"),
        P("fsdp"),
        P("fsdp", None, "tp"),
        P(None, ("tp", "fsdp")),
        P("tp", "fsdp"),
        P("fsdp"),
        P("fsdp", "tp"),
        P(("tp", "fsdp")),
        P("tp", "fsdp"),
        P("fsdp"),
        P("fsdp", "ctx", None),
    )
    given = (
        P("fsdp", "ctx", None),
        P("fsdp", "ctx", None),
        P("fsdp"),
        P("fsdp"),
        P("fsdp"),
        P("fsdp"),
        P("fsdp", None, "tp"),
        P(None, ("tp", "fsdp")),
        P("tp", "fsdp"),
        P("fsdp"),
        P("fsdp", "tp"),
        P(("tp", "fsdp")),
        P("tp", "fsdp"),
        P("fsdp"),
    )

    def run(*args):
        body = plane_local if splits_plane(mesh, args[0], args[7]) else gathered_local
        return jax.shard_map(
            body, mesh=mesh, in_specs=placed, out_specs=given, check_vma=False
        )(*args)

    return run
```

```python
import jax
import jax.numpy as jnp
from jax import lax
from jax.experimental import pallas as pl
from jax.experimental.pallas import tpu as pltpu
from jax.sharding import PartitionSpec as P

HD = 64
ROT = 16


EPS = 1e-05
ROPE_BASE = 10000.0


def rope_tables(offsets):
    half_dim = ROT // 2
    freq = ROPE_BASE ** (-(jnp.arange(half_dim, dtype=jnp.float32) * 2.0 / ROT))
    angle = offsets.astype(jnp.float32)[:, None] * freq[None, :]
    return (jnp.cos(angle)[:, None, :], jnp.sin(angle)[:, None, :])


def rotate(tensor, cosine, sine):
    half_dim = ROT // 2
    front = tensor[..., :half_dim]
    middle = tensor[..., half_dim:ROT]
    return jnp.concatenate(
        [front * cosine - middle * sine, middle * cosine + front * sine, tensor[..., ROT:]], axis=-1
    )


def unrotate(grads, cosine, sine):
    half_dim = ROT // 2
    front = grads[..., :half_dim]
    middle = grads[..., half_dim:ROT]
    return jnp.concatenate(
        [front * cosine + middle * sine, middle * cosine - front * sine, grads[..., ROT:]], axis=-1
    )


def normalize(rows):
    center = jnp.mean(rows, -1, keepdims=True)
    centred = rows - center
    spread = jnp.mean(centred * centred, -1, keepdims=True)
    rstd = lax.rsqrt(spread + EPS)
    return (centred * rstd, rstd)


def norm_back(upstream, normed, rstd, gain):
    scaled = upstream * gain
    return rstd * (
        scaled
        - jnp.mean(scaled, -1, keepdims=True)
        - normed * jnp.mean(scaled * normed, -1, keepdims=True)
    )


def masked_scores(query_blk, query_index, query_seg, keys, key_seg):
    scores = jnp.einsum(
        "qhe,khe->hqk", query_blk, keys, preferred_element_type=jnp.float32
    ) * HD ** (-0.5)
    key_index = jnp.arange(keys.shape[0], dtype=jnp.int32)
    allowed = (key_seg[None, :] == query_seg[:, None]) & (
        key_index[None, :] <= query_index[:, None]
    )
    return jnp.where(allowed[None], scores, -jnp.inf)


def gathered_local(
    tokens,
    segment_ids,
    positions,
    attention_gain,
    attention_shift,
    feedforward_gain,
    feedforward_shift,
    joint_weight,
    joint_bias,
    output_weight,
    output_bias,
    up_weight,
    up_bias,
    down_weight,
    down_bias,
    cotangent,
):
    f32 = jnp.float32
    bf16 = jnp.bfloat16
    scale = HD ** (-0.5)
    small = jnp.stack(
        [
            attention_gain,
            attention_shift,
            feedforward_gain,
            feedforward_shift,
            output_bias,
            down_bias,
        ]
    )
    full_joint, full_output, full_up, full_down, full_small, full_jbias, full_upbias = (
        lax.all_gather(joint_weight, "fsdp", axis=0, tiled=True),
        lax.all_gather(output_weight, "fsdp", axis=1, tiled=True),
        lax.all_gather(up_weight, "fsdp", axis=0, tiled=True),
        lax.all_gather(down_weight, "fsdp", axis=1, tiled=True),
        lax.all_gather(small, "fsdp", axis=1, tiled=True),
        lax.all_gather(joint_bias, "fsdp", axis=1, tiled=True),
        lax.all_gather(up_bias, "fsdp", axis=0, tiled=True),
    )
    params = full_small.astype(f32)
    gain_one = params[0]
    shift_one = params[1]
    gain_two = params[2]
    shift_two = params[3]
    rows = tokens[0].astype(f32)
    count_rows = rows.shape[0]
    local_width = joint_weight.shape[2]
    heads_here = local_width // HD
    normed, rstd = normalize(rows)
    first = (normed * gain_one + shift_one).astype(bf16)
    second = (normed * gain_two + shift_two).astype(bf16)
    joint = (
        jnp.einsum("nd,dpe->npe", first, full_joint, preferred_element_type=f32)
        + full_jbias.astype(f32)[None]
    )
    cosine, sine = rope_tables(positions[0])
    queries = rotate(joint[:, 0].reshape(count_rows, heads_here, HD), cosine, sine).astype(bf16)
    keys_here = rotate(joint[:, 1].reshape(count_rows, heads_here, HD), cosine, sine).astype(bf16)
    values_here = joint[:, 2].reshape(count_rows, heads_here, HD).astype(bf16)
    seg_here = segment_ids[0]
    all_keys, all_values, all_segs = (
        lax.all_gather(keys_here, "ctx", axis=0, tiled=True),
        lax.all_gather(values_here, "ctx", axis=0, tiled=True),
        lax.all_gather(seg_here.astype(bf16), "ctx", axis=0, tiled=True),
    )
    key_seg = all_segs.astype(f32)
    query_seg = seg_here.astype(f32)
    query_index = lax.axis_index("ctx") * count_rows + jnp.arange(count_rows, dtype=jnp.int32)
    block = min(512, count_rows)
    count_blocks = count_rows // block
    query_blocks = queries.reshape(count_blocks, block, heads_here, HD)
    index_blocks = query_index.reshape(count_blocks, block)
    seg_blocks = query_seg.reshape(count_blocks, block)

    def forward_block(args):
        query_blk, block_index, block_seg = args
        scores = masked_scores(query_blk, block_index, block_seg, all_keys, key_seg)
        top = jnp.max(scores, -1, keepdims=True)
        lse = top + jnp.log(jnp.sum(jnp.exp(scores - top), -1, keepdims=True))
        probs = jnp.exp(scores - lse).astype(bf16)
        mixed = jnp.einsum("hqk,khe->qhe", probs, all_values, preferred_element_type=f32)
        return (mixed, lse[..., 0])

    context32, lse_all = lax.map(forward_block, (query_blocks, index_blocks, seg_blocks))
    context32 = context32.reshape(count_rows, local_width)
    context = context32.astype(bf16)
    upper = jnp.dot(second, full_up, preferred_element_type=f32) + full_upbias.astype(f32)
    activated = jax.nn.gelu(upper, approximate=False).astype(bf16)
    partial_value = jnp.dot(context, full_output, preferred_element_type=f32) + jnp.dot(
        activated, full_down, preferred_element_type=f32
    )
    mixed_all = lax.psum(partial_value, "tp")
    result = rows + mixed_all + params[4] + params[5]
    back_joint, back_output, back_up, back_down = (
        lax.all_gather(joint_weight, "fsdp", axis=0, tiled=True),
        lax.all_gather(output_weight, "fsdp", axis=1, tiled=True),
        lax.all_gather(up_weight, "fsdp", axis=0, tiled=True),
        lax.all_gather(down_weight, "fsdp", axis=1, tiled=True),
    )
    cot = cotangent[0]
    cot_b = cot.astype(bf16)
    grad_output_w = jnp.dot(context.T, cot_b, preferred_element_type=f32)
    bias_sum = jnp.sum(cot, 0)
    grad_down_w = jnp.dot(activated.T, cot_b, preferred_element_type=f32)
    d_act = jnp.einsum("nd,fd->nf", cot_b, back_down, preferred_element_type=f32)
    unused, gelu_back = jax.vjp(lambda value: jax.nn.gelu(value, approximate=False), upper)
    d_upper = gelu_back(d_act)[0]
    d_upper_b = d_upper.astype(bf16)
    grad_up_w = jnp.dot(second.T, d_upper_b, preferred_element_type=f32)
    grad_up_b = jnp.sum(d_upper, 0)
    d_second_part = jnp.einsum("nf,df->nd", d_upper_b, back_up, preferred_element_type=f32)
    d_context = (
        jnp.einsum("nd,wd->nw", cot_b, back_output, preferred_element_type=f32)
        .astype(bf16)
        .reshape(count_rows, heads_here, HD)
    )
    delta = jnp.sum(d_context.astype(f32) * context32.reshape(count_rows, heads_here, HD), -1)
    dctx_blocks = d_context.reshape(count_blocks, block, heads_here, HD)

    def backward_block(args):
        query_blk, block_index, block_seg, dctx_blk, delta_blk, lse_blk = args
        scores = masked_scores(query_blk, block_index, block_seg, all_keys, key_seg)
        probs = jnp.exp(scores - lse_blk[..., None]).astype(bf16)
        d_probs = jnp.einsum("qhe,khe->hqk", dctx_blk, all_values, preferred_element_type=f32)
        d_scores = (probs.astype(f32) * (d_probs - jnp.transpose(delta_blk)[..., None])).astype(
            bf16
        )
        d_query_blk = (
            jnp.einsum("hqk,khe->qhe", d_scores, all_keys, preferred_element_type=f32) * scale
        )
        return (probs, d_scores, d_query_blk)

    probs_all, dscores_all, d_queries = lax.map(
        backward_block,
        (
            query_blocks,
            index_blocks,
            seg_blocks,
            dctx_blocks,
            delta.reshape(count_blocks, block, heads_here),
            lse_all,
        ),
    )
    d_queries = d_queries.reshape(count_rows, heads_here, HD)
    key_part = (
        jnp.einsum("bhqk,bqhe->khe", dscores_all, query_blocks, preferred_element_type=f32) * scale
    )
    value_part = jnp.einsum("bhqk,bqhe->khe", probs_all, dctx_blocks, preferred_element_type=f32)
    key_value = lax.psum_scatter(
        jnp.concatenate(
            [
                key_part.reshape(count_rows * lax.axis_size("ctx"), local_width),
                value_part.reshape(count_rows * lax.axis_size("ctx"), local_width),
            ],
            axis=1,
        ),
        "ctx",
        scatter_dimension=0,
        tiled=True,
    )
    d_keys = key_value[:, :local_width].reshape(count_rows, heads_here, HD)
    d_values = key_value[:, local_width:]
    d_joint = jnp.stack(
        [
            unrotate(d_queries, cosine, sine).reshape(count_rows, local_width),
            unrotate(d_keys, cosine, sine).reshape(count_rows, local_width),
            d_values,
        ],
        axis=1,
    )
    d_joint_b = d_joint.astype(bf16)
    grad_joint_w = jnp.einsum("nd,npe->dpe", first, d_joint_b, preferred_element_type=f32)
    grad_joint_b = jnp.sum(d_joint, 0)
    d_first_part = jnp.einsum("npe,dpe->nd", d_joint_b, back_joint, preferred_element_type=f32)
    d_first, d_second = lax.psum((d_first_part, d_second_part), "tp")
    norm_stats = jnp.stack(
        [
            jnp.sum(d_first * normed, 0),
            jnp.sum(d_first, 0),
            jnp.sum(d_second * normed, 0),
            jnp.sum(d_second, 0),
        ]
    )
    tokens_grad = (
        cot
        + norm_back(d_first, normed, rstd, gain_one)
        + norm_back(d_second, normed, rstd, gain_two)
    )
    grad_small = jnp.concatenate([norm_stats, bias_sum[None], bias_sum[None]], axis=0)
    share_joint, share_output, share_up, share_down, share_small, share_jbias, share_upbias = (
        lax.psum_scatter(grad_joint_w, ("fsdp", "ctx"), scatter_dimension=0, tiled=True),
        lax.psum_scatter(grad_output_w, ("fsdp", "ctx"), scatter_dimension=1, tiled=True),
        lax.psum_scatter(grad_up_w, ("fsdp", "ctx"), scatter_dimension=0, tiled=True),
        lax.psum_scatter(grad_down_w, ("fsdp", "ctx"), scatter_dimension=1, tiled=True),
        lax.psum_scatter(grad_small, ("fsdp", "ctx"), scatter_dimension=1, tiled=True),
        lax.psum_scatter(grad_joint_b, ("fsdp", "ctx"), scatter_dimension=1, tiled=True),
        lax.psum_scatter(grad_up_b, ("fsdp", "ctx"), scatter_dimension=0, tiled=True),
    )
    owned = (
        lax.all_gather(share_joint, "ctx", axis=0, tiled=True),
        lax.all_gather(share_output, "ctx", axis=1, tiled=True),
        lax.all_gather(share_up, "ctx", axis=0, tiled=True),
        lax.all_gather(share_down, "ctx", axis=1, tiled=True),
        lax.all_gather(share_small, "ctx", axis=1, tiled=True),
        lax.all_gather(share_jbias, "ctx", axis=1, tiled=True),
        lax.all_gather(share_upbias, "ctx", axis=0, tiled=True),
    )
    owned_joint, owned_output, owned_up, owned_down, owned_small, owned_jbias, owned_upbias = owned
    return (
        result[None],
        tokens_grad[None],
        owned_small[0],
        owned_small[1],
        owned_small[2],
        owned_small[3],
        owned_joint,
        owned_jbias,
        owned_output,
        owned_small[4],
        owned_up,
        owned_upbias,
        owned_down,
        owned_small[5],
    )


NEG = -1e30


def attention_body(
    heads, flips, place_ref, *refs,
):
    f32 = jnp.float32
    bf16 = jnp.bfloat16
    ins, refs = refs[:flips], refs[flips:]
    kseg_ref, qseg_ref, refs = refs[0], refs[1], refs[2:]
    outs, refs = refs[:flips], refs[flips:]
    x_ref, y_ref, kt_ref, vt_ref, s_ref, e_ref, dk_acc, dv_acc = refs
    step = pl.program_id(0)
    place = place_ref[0]
    rows = s_ref.shape[2]
    width = dk_acc.shape[1]
    chunks, _, chunk = kt_ref.shape
    hd = width // heads
    span = ins[0].shape[0]

    def spot(flip):
        return pl.ds(pl.multiple_of((place ^ flip) * span, span), span)

    k_ref = x_ref.at[:, width : 2 * width]
    v_ref = x_ref.at[:, 2 * width : 3 * width]

    @pl.when(step == 0)
    def _():
        for flip in range(flips):
            x_ref[spot(flip), :] = ins[flip][...]
        for c in range(chunks):
            part = pl.ds(c * chunk, chunk)
            kt_ref[c] = k_ref[part, :].astype(f32).T.astype(bf16)
            vt_ref[c] = v_ref[part, :].astype(f32).T.astype(bf16)
        dk_acc[...] = jnp.zeros_like(dk_acc)
        dv_acc[...] = jnp.zeros_like(dv_acc)

    here = pl.ds(pl.multiple_of(step * rows, rows), rows)
    used = ((step + 1) * rows + chunk - 1) // chunk
    q = x_ref[here, :width]
    q_t = q.astype(f32).T
    dc_t = x_ref[here, 3 * width :].astype(f32).T
    row_head = lax.broadcasted_iota(jnp.int32, (width, rows), 0) // hd
    lane_head = lax.broadcasted_iota(jnp.int32, (rows, width), 1) // hd
    q_heads_t = [jnp.where(row_head == h, q_t, 0.0).astype(bf16) for h in range(heads)]
    q_heads = [jnp.where(lane_head == h, q, jnp.zeros_like(q)) for h in range(heads)]
    qseg = qseg_ref[...]
    query = step * rows + lax.broadcasted_iota(jnp.int32, (1, rows), 1)
    key_base = lax.broadcasted_iota(jnp.int32, (chunk, 1), 0)

    def score(j, tops):
        part = pl.ds(pl.multiple_of(j * chunk, chunk), chunk)
        keys = k_ref[part, :]
        allowed = (kseg_ref[part, :] == qseg) & (key_base + j * chunk <= query)
        out = []
        for h in range(heads):
            s = jnp.dot(keys, q_heads_t[h], preferred_element_type=f32)
            s = jnp.where(allowed, s, NEG)
            s_ref[h, part, :] = s
            out.append(jnp.maximum(tops[h], jnp.max(s, 0, keepdims=True)))
        return tuple(out)

    tops = lax.fori_loop(
        0, used, score, tuple(jnp.full((1, rows), NEG, f32) for _ in range(heads))
    )

    def mix(j, carry):
        part = pl.ds(pl.multiple_of(j * chunk, chunk), chunk)
        values_t = vt_ref[j]
        out = []
        for h in range(heads):
            total, acc = carry[h]
            e = jnp.exp(s_ref[h, part, :] - tops[h])
            total = total + jnp.sum(e, 0, keepdims=True)
            e = e.astype(bf16)
            e_ref[h, part, :] = e
            acc = acc + jnp.dot(
                values_t[h * hd : (h + 1) * hd, :], e, preferred_element_type=f32
            )
            out.append((total, acc))
        return tuple(out)

    mixed = lax.fori_loop(
        0,
        used,
        mix,
        tuple((jnp.zeros((1, rows), f32), jnp.zeros((hd, rows), f32)) for _ in range(heads)),
    )
    ctx_parts, dcn_parts, deltas = [], [], []
    for h in range(heads):
        total, acc = mixed[h]
        inv = 1.0 / total
        ctx_h = acc * inv
        dc_h = dc_t[h * hd : (h + 1) * hd, :]
        deltas.append(jnp.sum(ctx_h * dc_h, 0, keepdims=True) * inv)
        ctx_parts.append(ctx_h)
        dcn_parts.append(dc_h * inv)
    y_ref[here, :width] = jnp.concatenate(ctx_parts, 0).T.astype(bf16)
    dcn_t = jnp.concatenate(dcn_parts, 0)
    dcn = dcn_t.T
    dcn_heads_t = [jnp.where(row_head == h, dcn_t, 0.0).astype(bf16) for h in range(heads)]
    dcn_heads = [jnp.where(lane_head == h, dcn, 0.0).astype(bf16) for h in range(heads)]

    def back(j, carry):
        part = pl.ds(pl.multiple_of(j * chunk, chunk), chunk)
        values = v_ref[part, :]
        keys_t = kt_ref[j]
        dk = dk_acc[part, :]
        dv = dv_acc[part, :]
        out = []
        for h in range(heads):
            e = e_ref[h, part, :]
            dp = jnp.dot(values, dcn_heads_t[h], preferred_element_type=f32)
            ds = (e.astype(f32) * (dp - deltas[h])).astype(bf16)
            out.append(
                carry[h]
                + jnp.dot(keys_t[h * hd : (h + 1) * hd, :], ds, preferred_element_type=f32)
            )
            dk = dk + jnp.dot(ds, q_heads[h], preferred_element_type=f32)
            dv = dv + jnp.dot(e, dcn_heads[h], preferred_element_type=f32)
        dk_acc[part, :] = dk
        dv_acc[part, :] = dv
        return tuple(out)

    dq = lax.fori_loop(
        0, used, back, tuple(jnp.zeros((hd, rows), f32) for _ in range(heads))
    )
    y_ref[here, width : 2 * width] = (jnp.concatenate(dq, 0).T * HD ** (-0.5)).astype(bf16)

    @pl.when(step == pl.num_programs(0) - 1)
    def _():
        y_ref[:, 2 * width : 3 * width] = dk_acc[...].astype(bf16)
        y_ref[:, 3 * width :] = dv_acc[...].astype(bf16)
        for flip in range(flips):
            outs[flip][...] = y_ref[spot(flip), :]


def attention(blocks, seg, place, block=256, chunk=256):
    flips = len(blocks)
    span, columns = blocks[0].shape
    count, width = span * flips, columns // 4
    heads = width // HD
    bf16 = jnp.bfloat16
    f32 = jnp.float32
    pairs = count * (count + block) // 2 * heads
    whole = pl.BlockSpec((span, columns), lambda i, p: (0, 0))
    return pl.pallas_call(
        lambda *refs: attention_body(heads, flips, *refs),
        grid_spec=pltpu.PrefetchScalarGridSpec(
            num_scalar_prefetch=1,
            grid=(count // block,),
            in_specs=[whole] * flips
            + [
                pl.BlockSpec((count, 1), lambda i, p: (0, 0)),
                pl.BlockSpec((1, block), lambda i, p: (0, i)),
            ],
            out_specs=[whole] * flips,
            scratch_shapes=[
                pltpu.VMEM((count, columns), bf16),
                pltpu.VMEM((count, columns), bf16),
                pltpu.VMEM((count // chunk, width, chunk), bf16),
                pltpu.VMEM((count // chunk, width, chunk), bf16),
                pltpu.VMEM((heads, count, block), f32),
                pltpu.VMEM((heads, count, block), bf16),
                pltpu.VMEM((count, width), f32),
                pltpu.VMEM((count, width), f32),
            ],
        ),
        out_shape=[jax.ShapeDtypeStruct((span, columns), bf16)] * flips,
        compiler_params=pltpu.CompilerParams(vmem_limit_bytes=48 * 1024 * 1024),
        cost_estimate=pl.CostEstimate(
            flops=10 * pairs * HD * 3, bytes_accessed=count * width * 16, transcendentals=pairs
        ),
        name="attention",
    )(place.reshape(1), *blocks, seg[:, None], seg[None, :])


def norm_body(core_ref, mine_ref, other_ref, params_ref, first_ref, second_ref, normed_ref):
    core = core_ref[0]
    f32 = jnp.float32
    for source, slot in ((mine_ref, core), (other_ref, 1 - core)):
        normed, _ = normalize(source[0].astype(f32))
        normed_ref[0, slot] = normed.astype(jnp.bfloat16)
        first_ref[0, slot] = (normed * params_ref[0:1] + params_ref[1:2]).astype(jnp.bfloat16)
        second_ref[0, slot] = (normed * params_ref[2:3] + params_ref[3:4]).astype(jnp.bfloat16)


def merge_body(core_ref, mine_ref, other_ref, out_ref):
    core = core_ref[0]
    out_ref[0, core] = mine_ref[0]
    out_ref[0, 1 - core] = other_ref[0]


def both_cores(body, mine, core, params, results):
    size, half, cols = mine.shape
    other = partner(mine, "tp", 1)
    side = pl.BlockSpec((1, half, cols), lambda i, c: (i, 0, 0))
    out = pl.BlockSpec((1, 2, half, cols), lambda i, c: (i, 0, 0, 0))
    extra = [pl.BlockSpec(p.shape, lambda i, c: (0, 0)) for p in params]
    made = pl.pallas_call(
        body,
        grid_spec=pltpu.PrefetchScalarGridSpec(
            num_scalar_prefetch=1,
            grid=(size,),
            in_specs=[side, side] + extra,
            out_specs=[out] * results,
        ),
        out_shape=[jax.ShapeDtypeStruct((size, 2, half, cols), mine.dtype)] * results,
        compiler_params=pltpu.CompilerParams(vmem_limit_bytes=32 * 1024 * 1024),
        cost_estimate=pl.CostEstimate(
            flops=size * half * cols * 20,
            bytes_accessed=size * half * cols * 4 * (1 + results),
            transcendentals=0,
        ),
        name=body.__name__,
    )(core.reshape(1), mine, other, *params)
    return [x.reshape(size * 2 * half, cols) for x in made]


def partner(tensor, axis, flip):
    size = lax.axis_size(axis)
    return lax.ppermute(tensor, axis, [(s, s ^ flip) for s in range(size)])


def pick(tensor, index, size, dim=0):
    return lax.dynamic_slice_in_dim(tensor, index * size, size, dim)


def swap(tensor, axis):
    return lax.all_to_all(tensor, axis, 0, 0)


def gather(block, axis):
    return swap(jnp.broadcast_to(block[None], (lax.axis_size(axis),) + block.shape), axis)


def double_up(block, axis, order):
    held = block[None]
    bits = []
    for bit in order:
        held = jnp.stack([held, partner(held, axis, 1 << bit)], 0)
        bits.insert(0, bit)
    levels = len(order)
    held = held.reshape((2,) * levels + block.shape)
    turn = [bits.index(bit) for bit in reversed(range(levels))]
    held = held.transpose(turn + list(range(levels, levels + block.ndim)))
    return held.reshape((2**levels,) + block.shape)


def chip_start(partial, size):
    f32 = jnp.float32
    core = lax.axis_index("tp")
    halves = partial.reshape(size, 2, -1, partial.shape[1])
    away = lax.dynamic_index_in_dim(halves, 1 - core, 1, keepdims=False)
    kept = lax.dynamic_index_in_dim(halves, core, 1, keepdims=False)
    return (kept.astype(f32) + partner(away, "tp", 1).astype(f32)).astype(partial.dtype)


def chip_finish(sending):
    f32 = jnp.float32
    total = sending[0].astype(f32)
    for flip in range(1, sending.shape[0]):
        total = total + partner(sending[flip], "fsdp", flip).astype(f32)
    return total


def chip_join(mine):
    core = lax.axis_index("tp")
    other = partner(mine, "tp", 1)
    low = jnp.where(core == 0, mine, other)
    high = jnp.where(core == 0, other, mine)
    return jnp.concatenate([low, high], 0)


def pack_wide(up, down, out, low, chips, part):
    span = down.shape[3] // chips
    for chip in range(chips):
        out[0, chip, :part, :] = up[chip, 0, low]
        for half in range(2):
            out[0, chip, part:, half * span : (half + 1) * span] = down[
                0, low, half * part : (half + 1) * part, chip * span : (chip + 1) * span
            ]


def pack_heads(joint, outw, out, low, chips, part):
    width = joint.shape[4]
    span = outw.shape[3] // chips // 2
    rows = part // 2
    for chip in range(chips):
        out[0, chip, :, :width] = joint[chip, 0, low]
        for half in range(2):
            begin = (2 * chip + half) * span
            out[0, chip, half * rows : (half + 1) * rows, width:] = outw[
                0, low, :, begin : begin + span
            ]


def pack(body, wide, tall, rows, chips, place):
    bf16 = jnp.bfloat16
    depth = 4
    part = wide.shape[0] // chips // depth
    cols = part * 8
    wide = wide.reshape(chips, 2, 2, part, wide.shape[1])
    tall = tall.reshape(2, 2, tall.shape[0] // depth, tall.shape[1])

    def run(place_ref, wide_ref, tall_ref, kept_ref, away_ref):
        side = place_ref[0] & 1
        body(wide_ref, tall_ref, kept_ref, side, chips, part)
        body(wide_ref, tall_ref, away_ref, 1 - side, chips, part)

    made = jax.ShapeDtypeStruct((2, chips, rows, cols), bf16)
    out = pl.BlockSpec((1, chips, rows, cols), lambda i, p: (i, 0, 0, 0))
    return pl.pallas_call(
        run,
        grid_spec=pltpu.PrefetchScalarGridSpec(
            num_scalar_prefetch=1,
            grid=(2,),
            in_specs=[
                pl.BlockSpec(
                    (chips, 1, 2, part, wide.shape[4]), lambda i, p: (0, i, 0, 0, 0)
                ),
                pl.BlockSpec((1,) + tall.shape[1:], lambda i, p: (i, 0, 0, 0)),
            ],
            out_specs=[out, out],
        ),
        out_shape=[made, made],
        compiler_params=pltpu.CompilerParams(vmem_limit_bytes=24 * 1024 * 1024),
        cost_estimate=pl.CostEstimate(
            flops=0, bytes_accessed=16 * chips * rows * cols, transcendentals=0
        ),
        name=body.__name__,
    )(place.reshape(1), wide, tall)


def unpack_wide(x, up, down, chips, part):
    f32 = jnp.float32
    span = down.shape[3]
    cols = x.shape[2]
    for chip in range(chips):
        up[:, chip * cols : (chip + 1) * cols] = x[chip, :part, :].astype(f32)
        for half in range(2):
            down[chip, 0, half * part : (half + 1) * part, :] = x[
                chip, part:, half * span : (half + 1) * span
            ].astype(f32)


def unpack_heads(x, joint, outw, chips, part):
    f32 = jnp.float32
    span = outw.shape[3] // 2
    rows = part // 2
    width = joint.shape[2] // chips
    for chip in range(chips):
        for kind in range(3):
            joint[kind, :, chip * width : (chip + 1) * width] = x[
                chip, :, kind * width : (kind + 1) * width
            ].astype(f32)
        for half in range(2):
            outw[chip, 0, :, half * span : (half + 1) * span] = x[
                chip, half * rows : (half + 1) * rows, 3 * width :
            ].astype(f32)


def unpack(body, blocks, wide, wide_block, tall, tall_block, place):
    f32 = jnp.float32
    chips, rows, cols = blocks[0].shape
    depth = len(blocks)
    whole = pl.BlockSpec((chips, rows, cols), lambda i, p: (0, 0, 0))

    def run(place_ref, *refs):
        for k in range(depth):

            @pl.when(pl.program_id(0) == k)
            def _(k=k):
                body(refs[k], refs[depth], refs[depth + 1], chips, cols // 8)

    def at(dim, count):
        return lambda i, p: tuple((p[0] ^ i) if d == dim else 0 for d in range(count))

    dim = len(wide) - 2
    return pl.pallas_call(
        run,
        grid_spec=pltpu.PrefetchScalarGridSpec(
            num_scalar_prefetch=1,
            grid=(depth,),
            in_specs=[whole] * depth,
            out_specs=[
                pl.BlockSpec(wide_block, at(dim, len(wide))),
                pl.BlockSpec(tall_block, at(1, len(tall))),
            ],
        ),
        out_shape=[jax.ShapeDtypeStruct(wide, f32), jax.ShapeDtypeStruct(tall, f32)],
        compiler_params=pltpu.CompilerParams(vmem_limit_bytes=24 * 1024 * 1024),
        cost_estimate=pl.CostEstimate(
            flops=0, bytes_accessed=6 * depth * chips * rows * cols, transcendentals=0
        ),
        name=body.__name__,
    )(place.reshape(1), *blocks)


def sum_slots(kept, away, gate=()):
    f32 = jnp.float32
    bf16 = jnp.bfloat16
    side = lax.axis_index("ctx") >> 1
    held = (kept.astype(f32) + partner(away, "ctx", 1).astype(f32)).astype(bf16)
    held = after(held, *gate)
    kept = lax.dynamic_index_in_dim(held, side, 0, keepdims=False)
    away = lax.dynamic_index_in_dim(held, 1 - side, 0, keepdims=False)
    return (kept.astype(f32) + partner(away, "ctx", 2).astype(f32)).astype(bf16)


def spread(held):
    far = partner(held, "ctx", 2)
    return [held, partner(held, "ctx", 1), far, partner(far, "ctx", 1)]


def after(tensor, *others):
    return lax.optimization_barrier((tensor,) + others)[0]


def plane_local(
    tokens,
    segment_ids,
    positions,
    attention_gain,
    attention_shift,
    feedforward_gain,
    feedforward_shift,
    joint_weight,
    joint_bias,
    output_weight,
    output_bias,
    up_weight,
    up_bias,
    down_weight,
    down_bias,
    cotangent,
):
    f32 = jnp.float32
    bf16 = jnp.bfloat16
    me, place, core = lax.axis_index("fsdp"), lax.axis_index("ctx"), lax.axis_index("tp")
    size = lax.axis_size("fsdp")
    depth = lax.axis_size("ctx")
    count, model = tokens.shape[1:]
    half_rows = count // 2
    rows = tokens[0].astype(f32)
    cot = cotangent[0]
    levels = list(range(size.bit_length() - 1))

    my_tokens = double_up(pick(tokens[0], core, half_rows), "fsdp", levels)
    my_cot = double_up(pick(cot, core, half_rows).astype(bf16), "fsdp", levels[::-1])
    width = joint_weight.shape[2] // size
    joint_w = swap(
        joint_weight.reshape(-1, 3, size, width).transpose(2, 0, 1, 3), "fsdp"
    ).reshape(model, 3, width)
    small = jnp.concatenate(
        [
            attention_gain,
            attention_shift,
            feedforward_gain,
            feedforward_shift,
            output_bias,
            down_bias,
        ]
    ).astype(f32)
    notes = jnp.concatenate([small, segment_ids[0].astype(f32), positions[0].astype(f32)])
    packed = gather(
        after(notes, joint_w),
        ("fsdp", "ctx"),
    ).reshape(size, depth, -1)
    params = packed[:, 0, : small.size].reshape(size, 6, -1).transpose(1, 0, 2).reshape(6, model)
    seg_seq = lax.dynamic_index_in_dim(packed, place, 0, keepdims=False)
    seg_seq = seg_seq[:, small.size : small.size + count].reshape(-1)
    pos_here = lax.dynamic_index_in_dim(packed, place, 1, keepdims=False)[:, small.size + count :]
    pos_plane = jnp.concatenate(
        [lax.dynamic_index_in_dim(pos_here, me ^ k, 0, keepdims=False) for k in range(size)]
    )
    output_w = swap(after(output_weight, packed).reshape(size, width, -1), "fsdp")
    output_w = output_w.transpose(1, 0, 2).reshape(width, model)
    first, second, normed = both_cores(norm_body, my_tokens, core, [params[:4]], 3)
    (cot_b,) = both_cores(merge_body, my_cot, core, [], 1)
    hidden = up_weight.shape[1] // size
    up_send = up_weight.reshape(-1, size, hidden).transpose(1, 0, 2)
    up_w = swap(after(up_send, output_w, first, cot_b), "fsdp")
    up_w = up_w.reshape(model, hidden)
    down_w = swap(after(down_weight, up_w).reshape(size, hidden, -1), "fsdp")
    down_w = down_w.transpose(1, 0, 2).reshape(hidden, model)


    lane = jnp.arange(width, dtype=jnp.int32) % HD
    half = ROT // 2
    freq = jnp.where(
        lane < ROT, ROPE_BASE ** (-((lane % half).astype(f32) * 2.0 / ROT)), 0.0
    )
    angle = pos_plane[:, None] * freq[None, :]
    cosine = jnp.cos(angle)
    sine = jnp.sin(angle) * jnp.where(lane < half, -1.0, 1.0)[None, :]
    source = jnp.arange(width, dtype=jnp.int32)
    source = jnp.where(lane < half, source + half, jnp.where(lane < ROT, source - half, -1))
    turn = (jnp.arange(width, dtype=jnp.int32)[:, None] == source[None, :]).astype(bf16)

    joint_flat = joint_w.reshape(model, 3 * width)
    bias = joint_bias.astype(f32)
    joint = jnp.dot(first, joint_flat, preferred_element_type=f32) + bias.reshape(-1)[None]
    swapped_w = jnp.einsum("dpe,ef->dpf", joint_w[:, :2], turn, preferred_element_type=bf16)
    swapped_b = jnp.dot(joint_bias[:2], turn, preferred_element_type=f32)
    swapped = (
        jnp.dot(first, swapped_w.reshape(model, 2 * width), preferred_element_type=f32)
        + swapped_b.reshape(-1)[None]
    )
    scale = HD ** (-0.5)
    queries = (joint[:, :width] * cosine + swapped[:, :width] * sine) * scale
    keys = joint[:, width : 2 * width] * cosine + swapped[:, width:] * sine
    d_context = jnp.einsum("nd,wd->nw", cot_b, output_w, preferred_element_type=f32)
    sending = jnp.concatenate([queries, keys, joint[:, 2 * width :], d_context], 1).astype(bf16)
    blocks = []
    for flip in range(depth):
        block = pick(sending, me ^ place ^ flip, count)
        blocks.append(partner(block, "ctx", flip) if flip else block)
    second, up_w = lax.optimization_barrier((second, up_w, sending))[:2]

    upper = jnp.dot(second, up_w, preferred_element_type=f32) + up_bias.astype(f32)[None]
    gelu, gelu_back = jax.vjp(lambda value: jax.nn.gelu(value, approximate=False), upper)
    activated = gelu.astype(bf16)
    d_act = jnp.einsum("nd,fd->nf", cot_b, down_w, preferred_element_type=f32)
    d_upper = gelu_back(d_act)[0]
    d_upper_b = d_upper.astype(bf16)
    grad_up_b = jnp.sum(d_upper, 0)
    moment_up = jnp.dot(normed.T, d_upper_b, preferred_element_type=f32)
    d_upper_sum = jnp.sum(d_upper_b.astype(f32), 0)
    grad_up_w = (
        params[2][:, None] * moment_up + params[3][:, None] * d_upper_sum[None, :]
    ).astype(bf16)
    up_f32 = up_w.astype(f32)
    gain_two_grad = jnp.sum(up_f32 * moment_up, 1)
    shift_two_grad = jnp.sum(up_f32 * d_upper_sum[None, :], 1)
    grad_down_w = jnp.dot(activated.T, cot_b, preferred_element_type=f32).astype(bf16)
    part = model // size // depth
    kept, away = pack(pack_wide, grad_up_w, grad_down_w, 2 * part, size, place)
    held = (kept, away)
    blocks = lax.optimization_barrier((tuple(blocks), kept, away))[0]
    made = attention(blocks, seg_seq, place)
    kept, away = held
    held = swap(sum_slots(kept, away), "fsdp")
    owned_up, owned_down = unpack(
        unpack_wide,
        spread(held),
        (model // size, up_weight.shape[1]),
        (part, up_weight.shape[1]),
        (size, depth, 2 * part, 2 * width),
        (size, 1, 2 * part, 2 * width),
        place,
    )
    owned_down = owned_down.reshape(down_weight.shape)
    gained = (up_f32 * params[2][:, None]).astype(bf16)
    upstream_two = jnp.einsum("nf,df->nd", d_upper_b, gained, preferred_element_type=f32)
    upstream_two = upstream_two.astype(bf16)
    mixed_two = jnp.dot(activated, down_w, preferred_element_type=f32).astype(bf16)

    back = jnp.zeros(sending.shape, bf16)
    for flip in range(depth):
        block = partner(made[flip], "ctx", flip) if flip else made[flip]
        back = lax.dynamic_update_slice_in_dim(back, block, (me ^ place ^ flip) * count, 0)
    context = back[:, :width]
    d_qk = back[:, width : 3 * width]
    grad_output_w = jnp.dot(context.T, cot_b, preferred_element_type=f32).astype(bf16)

    d_swapped = jnp.einsum(
        "npe,ef->npf", d_qk.reshape(-1, 2, width), turn, preferred_element_type=f32
    ).reshape(-1, 2 * width)
    cosines = jnp.concatenate([cosine, cosine], 1)
    sines = jnp.concatenate([sine, sine], 1)
    d_joint = jnp.concatenate(
        [d_qk.astype(f32) * cosines - d_swapped * sines, back[:, 3 * width :].astype(f32)], 1
    )
    d_joint_b = d_joint.astype(bf16)
    grad_joint_b = jnp.sum(d_joint, 0)
    moment_joint = jnp.dot(normed.T, d_joint_b, preferred_element_type=f32)
    d_joint_sum = jnp.sum(d_joint_b.astype(f32), 0)
    grad_joint_w = (
        params[0][:, None] * moment_joint + params[1][:, None] * d_joint_sum[None, :]
    ).astype(bf16)
    kept, away = pack(pack_heads, grad_joint_w, grad_output_w, part, size, place)
    context, d_joint_b = lax.optimization_barrier((context, d_joint_b, kept, away))[:2]
    mixed = jnp.dot(context, output_w, preferred_element_type=f32) + mixed_two.astype(f32)
    sending_result = chip_start(mixed.astype(bf16), size)
    joint_f32 = joint_flat.astype(f32)
    gained = (joint_f32 * params[0][:, None]).astype(bf16)
    upstream = jnp.einsum("ne,de->nd", d_joint_b, gained, preferred_element_type=f32)
    sending_up = chip_start((upstream + upstream_two.astype(f32)).astype(bf16), size)
    held = sum_slots(kept, away, (sending_result, sending_up))
    held = swap(held, "fsdp")
    owned_joint, owned_output = unpack(
        unpack_heads,
        spread(held),
        (3, model // size, joint_weight.shape[2]),
        (3, part, joint_weight.shape[2]),
        (size, depth, part // 2, 2 * width),
        (size, 1, part // 2, 2 * width),
        place,
    )
    owned_joint = owned_joint.transpose(1, 0, 2)
    owned_output = owned_output.reshape(output_weight.shape)

    my_rows = pick(rows, core, half_rows)
    result = chip_join(my_rows + chip_finish(sending_result) + params[4] + params[5])
    normed_here, rstd = normalize(my_rows)
    upstream = chip_finish(sending_up)
    tokens_grad = chip_join(
        pick(cot, core, half_rows)
        + rstd
        * (
            upstream
            - jnp.mean(upstream, -1, keepdims=True)
            - normed_here * jnp.mean(upstream * normed_here, -1, keepdims=True)
        )
    )
    stats = jnp.stack(
        [
            jnp.sum(joint_f32 * moment_joint, 1),
            jnp.sum(joint_f32 * d_joint_sum[None, :], 1),
            gain_two_grad,
            shift_two_grad,
            jnp.sum(pick(cot, core, half_rows), 0),
        ]
    )
    stats = jnp.sum(swap(stats.reshape(5, size, -1).transpose(1, 0, 2), "fsdp"), 0)
    packed = jnp.concatenate([stats.reshape(-1), grad_joint_b, grad_up_b])
    packed = gather(packed, ("ctx", "tp")).reshape(depth, 2, -1)
    owned = jnp.sum(packed[:, :, : stats.size], (0, 1)).reshape(stats.shape)
    biases = jnp.sum(packed[:, :, stats.size :], 0)
    biases = lax.dynamic_index_in_dim(biases, core, 0, keepdims=False)
    owned_jbias = biases[: 3 * width].reshape(3, width)
    owned_upbias = biases[3 * width :]
    return (
        result[None],
        tokens_grad[None],
        owned[0],
        owned[1],
        owned[2],
        owned[3],
        owned_joint,
        owned_jbias,
        owned_output,
        owned[4],
        owned_up,
        owned_upbias,
        owned_down,
        owned[4],
    )


def splits_plane(mesh, tokens, joint_weight, up_weight):
    size, depth, cores = mesh.shape["fsdp"], mesh.shape["ctx"], mesh.shape["tp"]
    width = joint_weight.shape[2] // (size * cores)
    return (
        size == depth == tokens.shape[0] == 4
        and cores == 2
        and width % 128 == 0
        and tokens.shape[2] == 2 * size * width
        and up_weight.shape[1] == 4 * size * cores * width
        and tokens.shape[1] // depth % 256 == 0
    )


def solution(mesh):
    placed = (
        P("fsdp", "ctx", None),
        P("fsdp", "ctx"),
        P("fsdp", "ctx"),
        P("fsdp"),
        P("fsdp"),
        P("fsdp"),
        P("fsdp"),
        P("fsdp", None, "tp"),
        P(None, ("tp", "fsdp")),
        P("tp", "fsdp"),
        P("fsdp"),
        P("fsdp", "tp"),
        P(("tp", "fsdp")),
        P("tp", "fsdp"),
        P("fsdp"),
        P("fsdp", "ctx", None),
    )
    given = (
        P("fsdp", "ctx", None),
        P("fsdp", "ctx", None),
        P("fsdp"),
        P("fsdp"),
        P("fsdp"),
        P("fsdp"),
        P("fsdp", None, "tp"),
        P(None, ("tp", "fsdp")),
        P("tp", "fsdp"),
        P("fsdp"),
        P("fsdp", "tp"),
        P(("tp", "fsdp")),
        P("tp", "fsdp"),
        P("fsdp"),
    )

    def run(*args):
        body = plane_local if splits_plane(mesh, args[0], args[7], args[11]) else gathered_local
        return jax.shard_map(
            body, mesh=mesh, in_specs=placed, out_specs=given, check_vma=False
        )(*args)

    return run
```

```python
import jax
import jax.numpy as jnp
from jax import lax
from jax.experimental import pallas as pl
from jax.experimental.pallas import tpu as pltpu
from jax.sharding import PartitionSpec as P

HD = 64
ROT = 16


EPS = 1e-05
ROPE_BASE = 10000.0


def rope_tables(offsets):
    half_dim = ROT // 2
    freq = ROPE_BASE ** (-(jnp.arange(half_dim, dtype=jnp.float32) * 2.0 / ROT))
    angle = offsets.astype(jnp.float32)[:, None] * freq[None, :]
    return (jnp.cos(angle)[:, None, :], jnp.sin(angle)[:, None, :])


def rotate(tensor, cosine, sine):
    half_dim = ROT // 2
    front = tensor[..., :half_dim]
    middle = tensor[..., half_dim:ROT]
    return jnp.concatenate(
        [front * cosine - middle * sine, middle * cosine + front * sine, tensor[..., ROT:]], axis=-1
    )


def unrotate(grads, cosine, sine):
    half_dim = ROT // 2
    front = grads[..., :half_dim]
    middle = grads[..., half_dim:ROT]
    return jnp.concatenate(
        [front * cosine + middle * sine, middle * cosine - front * sine, grads[..., ROT:]], axis=-1
    )


def normalize(rows):
    center = jnp.mean(rows, -1, keepdims=True)
    centred = rows - center
    spread = jnp.mean(centred * centred, -1, keepdims=True)
    rstd = lax.rsqrt(spread + EPS)
    return (centred * rstd, rstd)


def norm_back(upstream, normed, rstd, gain):
    scaled = upstream * gain
    return rstd * (
        scaled
        - jnp.mean(scaled, -1, keepdims=True)
        - normed * jnp.mean(scaled * normed, -1, keepdims=True)
    )


def masked_scores(query_blk, query_index, query_seg, keys, key_seg):
    scores = jnp.einsum(
        "qhe,khe->hqk", query_blk, keys, preferred_element_type=jnp.float32
    ) * HD ** (-0.5)
    key_index = jnp.arange(keys.shape[0], dtype=jnp.int32)
    allowed = (key_seg[None, :] == query_seg[:, None]) & (
        key_index[None, :] <= query_index[:, None]
    )
    return jnp.where(allowed[None], scores, -jnp.inf)


def gathered_local(
    tokens,
    segment_ids,
    positions,
    attention_gain,
    attention_shift,
    feedforward_gain,
    feedforward_shift,
    joint_weight,
    joint_bias,
    output_weight,
    output_bias,
    up_weight,
    up_bias,
    down_weight,
    down_bias,
    cotangent,
):
    f32 = jnp.float32
    bf16 = jnp.bfloat16
    scale = HD ** (-0.5)
    small = jnp.stack(
        [
            attention_gain,
            attention_shift,
            feedforward_gain,
            feedforward_shift,
            output_bias,
            down_bias,
        ]
    )
    full_joint, full_output, full_up, full_down, full_small, full_jbias, full_upbias = (
        lax.all_gather(joint_weight, "fsdp", axis=0, tiled=True),
        lax.all_gather(output_weight, "fsdp", axis=1, tiled=True),
        lax.all_gather(up_weight, "fsdp", axis=0, tiled=True),
        lax.all_gather(down_weight, "fsdp", axis=1, tiled=True),
        lax.all_gather(small, "fsdp", axis=1, tiled=True),
        lax.all_gather(joint_bias, "fsdp", axis=1, tiled=True),
        lax.all_gather(up_bias, "fsdp", axis=0, tiled=True),
    )
    params = full_small.astype(f32)
    gain_one = params[0]
    shift_one = params[1]
    gain_two = params[2]
    shift_two = params[3]
    rows = tokens[0].astype(f32)
    count_rows = rows.shape[0]
    local_width = joint_weight.shape[2]
    heads_here = local_width // HD
    normed, rstd = normalize(rows)
    first = (normed * gain_one + shift_one).astype(bf16)
    second = (normed * gain_two + shift_two).astype(bf16)
    joint = (
        jnp.einsum("nd,dpe->npe", first, full_joint, preferred_element_type=f32)
        + full_jbias.astype(f32)[None]
    )
    cosine, sine = rope_tables(positions[0])
    queries = rotate(joint[:, 0].reshape(count_rows, heads_here, HD), cosine, sine).astype(bf16)
    keys_here = rotate(joint[:, 1].reshape(count_rows, heads_here, HD), cosine, sine).astype(bf16)
    values_here = joint[:, 2].reshape(count_rows, heads_here, HD).astype(bf16)
    seg_here = segment_ids[0]
    all_keys, all_values, all_segs = (
        lax.all_gather(keys_here, "ctx", axis=0, tiled=True),
        lax.all_gather(values_here, "ctx", axis=0, tiled=True),
        lax.all_gather(seg_here.astype(bf16), "ctx", axis=0, tiled=True),
    )
    key_seg = all_segs.astype(f32)
    query_seg = seg_here.astype(f32)
    query_index = lax.axis_index("ctx") * count_rows + jnp.arange(count_rows, dtype=jnp.int32)
    block = min(512, count_rows)
    count_blocks = count_rows // block
    query_blocks = queries.reshape(count_blocks, block, heads_here, HD)
    index_blocks = query_index.reshape(count_blocks, block)
    seg_blocks = query_seg.reshape(count_blocks, block)

    def forward_block(args):
        query_blk, block_index, block_seg = args
        scores = masked_scores(query_blk, block_index, block_seg, all_keys, key_seg)
        top = jnp.max(scores, -1, keepdims=True)
        lse = top + jnp.log(jnp.sum(jnp.exp(scores - top), -1, keepdims=True))
        probs = jnp.exp(scores - lse).astype(bf16)
        mixed = jnp.einsum("hqk,khe->qhe", probs, all_values, preferred_element_type=f32)
        return (mixed, lse[..., 0])

    context32, lse_all = lax.map(forward_block, (query_blocks, index_blocks, seg_blocks))
    context32 = context32.reshape(count_rows, local_width)
    context = context32.astype(bf16)
    upper = jnp.dot(second, full_up, preferred_element_type=f32) + full_upbias.astype(f32)
    activated = jax.nn.gelu(upper, approximate=False).astype(bf16)
    partial_value = jnp.dot(context, full_output, preferred_element_type=f32) + jnp.dot(
        activated, full_down, preferred_element_type=f32
    )
    mixed_all = lax.psum(partial_value, "tp")
    result = rows + mixed_all + params[4] + params[5]
    back_joint, back_output, back_up, back_down = (
        lax.all_gather(joint_weight, "fsdp", axis=0, tiled=True),
        lax.all_gather(output_weight, "fsdp", axis=1, tiled=True),
        lax.all_gather(up_weight, "fsdp", axis=0, tiled=True),
        lax.all_gather(down_weight, "fsdp", axis=1, tiled=True),
    )
    cot = cotangent[0]
    cot_b = cot.astype(bf16)
    grad_output_w = jnp.dot(context.T, cot_b, preferred_element_type=f32)
    bias_sum = jnp.sum(cot, 0)
    grad_down_w = jnp.dot(activated.T, cot_b, preferred_element_type=f32)
    d_act = jnp.einsum("nd,fd->nf", cot_b, back_down, preferred_element_type=f32)
    unused, gelu_back = jax.vjp(lambda value: jax.nn.gelu(value, approximate=False), upper)
    d_upper = gelu_back(d_act)[0]
    d_upper_b = d_upper.astype(bf16)
    grad_up_w = jnp.dot(second.T, d_upper_b, preferred_element_type=f32)
    grad_up_b = jnp.sum(d_upper, 0)
    d_second_part = jnp.einsum("nf,df->nd", d_upper_b, back_up, preferred_element_type=f32)
    d_context = (
        jnp.einsum("nd,wd->nw", cot_b, back_output, preferred_element_type=f32)
        .astype(bf16)
        .reshape(count_rows, heads_here, HD)
    )
    delta = jnp.sum(d_context.astype(f32) * context32.reshape(count_rows, heads_here, HD), -1)
    dctx_blocks = d_context.reshape(count_blocks, block, heads_here, HD)

    def backward_block(args):
        query_blk, block_index, block_seg, dctx_blk, delta_blk, lse_blk = args
        scores = masked_scores(query_blk, block_index, block_seg, all_keys, key_seg)
        probs = jnp.exp(scores - lse_blk[..., None]).astype(bf16)
        d_probs = jnp.einsum("qhe,khe->hqk", dctx_blk, all_values, preferred_element_type=f32)
        d_scores = (probs.astype(f32) * (d_probs - jnp.transpose(delta_blk)[..., None])).astype(
            bf16
        )
        d_query_blk = (
            jnp.einsum("hqk,khe->qhe", d_scores, all_keys, preferred_element_type=f32) * scale
        )
        return (probs, d_scores, d_query_blk)

    probs_all, dscores_all, d_queries = lax.map(
        backward_block,
        (
            query_blocks,
            index_blocks,
            seg_blocks,
            dctx_blocks,
            delta.reshape(count_blocks, block, heads_here),
            lse_all,
        ),
    )
    d_queries = d_queries.reshape(count_rows, heads_here, HD)
    key_part = (
        jnp.einsum("bhqk,bqhe->khe", dscores_all, query_blocks, preferred_element_type=f32) * scale
    )
    value_part = jnp.einsum("bhqk,bqhe->khe", probs_all, dctx_blocks, preferred_element_type=f32)
    key_value = lax.psum_scatter(
        jnp.concatenate(
            [
                key_part.reshape(count_rows * lax.axis_size("ctx"), local_width),
                value_part.reshape(count_rows * lax.axis_size("ctx"), local_width),
            ],
            axis=1,
        ),
        "ctx",
        scatter_dimension=0,
        tiled=True,
    )
    d_keys = key_value[:, :local_width].reshape(count_rows, heads_here, HD)
    d_values = key_value[:, local_width:]
    d_joint = jnp.stack(
        [
            unrotate(d_queries, cosine, sine).reshape(count_rows, local_width),
            unrotate(d_keys, cosine, sine).reshape(count_rows, local_width),
            d_values,
        ],
        axis=1,
    )
    d_joint_b = d_joint.astype(bf16)
    grad_joint_w = jnp.einsum("nd,npe->dpe", first, d_joint_b, preferred_element_type=f32)
    grad_joint_b = jnp.sum(d_joint, 0)
    d_first_part = jnp.einsum("npe,dpe->nd", d_joint_b, back_joint, preferred_element_type=f32)
    d_first, d_second = lax.psum((d_first_part, d_second_part), "tp")
    norm_stats = jnp.stack(
        [
            jnp.sum(d_first * normed, 0),
            jnp.sum(d_first, 0),
            jnp.sum(d_second * normed, 0),
            jnp.sum(d_second, 0),
        ]
    )
    tokens_grad = (
        cot
        + norm_back(d_first, normed, rstd, gain_one)
        + norm_back(d_second, normed, rstd, gain_two)
    )
    grad_small = jnp.concatenate([norm_stats, bias_sum[None], bias_sum[None]], axis=0)
    share_joint, share_output, share_up, share_down, share_small, share_jbias, share_upbias = (
        lax.psum_scatter(grad_joint_w, ("fsdp", "ctx"), scatter_dimension=0, tiled=True),
        lax.psum_scatter(grad_output_w, ("fsdp", "ctx"), scatter_dimension=1, tiled=True),
        lax.psum_scatter(grad_up_w, ("fsdp", "ctx"), scatter_dimension=0, tiled=True),
        lax.psum_scatter(grad_down_w, ("fsdp", "ctx"), scatter_dimension=1, tiled=True),
        lax.psum_scatter(grad_small, ("fsdp", "ctx"), scatter_dimension=1, tiled=True),
        lax.psum_scatter(grad_joint_b, ("fsdp", "ctx"), scatter_dimension=1, tiled=True),
        lax.psum_scatter(grad_up_b, ("fsdp", "ctx"), scatter_dimension=0, tiled=True),
    )
    owned = (
        lax.all_gather(share_joint, "ctx", axis=0, tiled=True),
        lax.all_gather(share_output, "ctx", axis=1, tiled=True),
        lax.all_gather(share_up, "ctx", axis=0, tiled=True),
        lax.all_gather(share_down, "ctx", axis=1, tiled=True),
        lax.all_gather(share_small, "ctx", axis=1, tiled=True),
        lax.all_gather(share_jbias, "ctx", axis=1, tiled=True),
        lax.all_gather(share_upbias, "ctx", axis=0, tiled=True),
    )
    owned_joint, owned_output, owned_up, owned_down, owned_small, owned_jbias, owned_upbias = owned
    return (
        result[None],
        tokens_grad[None],
        owned_small[0],
        owned_small[1],
        owned_small[2],
        owned_small[3],
        owned_joint,
        owned_jbias,
        owned_output,
        owned_small[4],
        owned_up,
        owned_upbias,
        owned_down,
        owned_small[5],
    )


NEG = -1e30


def attention_body(
    heads, flips, place_ref, *refs,
):
    f32 = jnp.float32
    bf16 = jnp.bfloat16
    ins, refs = refs[: 2 * flips], refs[2 * flips :]
    kseg_ref, qseg_ref, refs = refs[0], refs[1], refs[2:]
    outs, refs = refs[:flips], refs[flips:]
    x_ref, y_ref, kt_ref, vt_ref, s_ref, e_ref, dk_acc, dv_acc = refs
    step = pl.program_id(0)
    place = place_ref[0]
    rows = s_ref.shape[2]
    width = dk_acc.shape[1]
    chunks, _, chunk = kt_ref.shape
    hd = width // heads
    span = ins[0].shape[0]

    def spot(flip):
        return pl.ds(pl.multiple_of((place ^ flip) * span, span), span)

    k_ref = x_ref.at[:, width : 2 * width]
    v_ref = x_ref.at[:, 2 * width : 3 * width]

    @pl.when(step == 0)
    def _():
        for flip in range(flips):
            x_ref[spot(flip), : 3 * width] = ins[flip][...]
            x_ref[spot(flip), 3 * width :] = ins[flips + flip][...]
        for c in range(chunks):
            part = pl.ds(c * chunk, chunk)
            kt_ref[c] = k_ref[part, :].astype(f32).T.astype(bf16)
            vt_ref[c] = v_ref[part, :].astype(f32).T.astype(bf16)
        dk_acc[...] = jnp.zeros_like(dk_acc)
        dv_acc[...] = jnp.zeros_like(dv_acc)

    here = pl.ds(pl.multiple_of(step * rows, rows), rows)
    used = ((step + 1) * rows + chunk - 1) // chunk
    q = x_ref[here, :width]
    q_t = q.astype(f32).T
    dc_t = x_ref[here, 3 * width :].astype(f32).T
    row_head = lax.broadcasted_iota(jnp.int32, (width, rows), 0) // hd
    lane_head = lax.broadcasted_iota(jnp.int32, (rows, width), 1) // hd
    q_heads_t = [jnp.where(row_head == h, q_t, 0.0).astype(bf16) for h in range(heads)]
    q_heads = [jnp.where(lane_head == h, q, jnp.zeros_like(q)) for h in range(heads)]
    qseg = qseg_ref[...]
    query = step * rows + lax.broadcasted_iota(jnp.int32, (1, rows), 1)
    key_base = lax.broadcasted_iota(jnp.int32, (chunk, 1), 0)

    def score(j, tops):
        part = pl.ds(pl.multiple_of(j * chunk, chunk), chunk)
        keys = k_ref[part, :]
        allowed = (kseg_ref[part, :] == qseg) & (key_base + j * chunk <= query)
        out = []
        for h in range(heads):
            s = jnp.dot(keys, q_heads_t[h], preferred_element_type=f32)
            s = jnp.where(allowed, s, NEG)
            s_ref[h, part, :] = s
            out.append(jnp.maximum(tops[h], jnp.max(s, 0, keepdims=True)))
        return tuple(out)

    tops = lax.fori_loop(
        0, used, score, tuple(jnp.full((1, rows), NEG, f32) for _ in range(heads))
    )

    def mix(j, carry):
        part = pl.ds(pl.multiple_of(j * chunk, chunk), chunk)
        values_t = vt_ref[j]
        out = []
        for h in range(heads):
            total, acc = carry[h]
            e = jnp.exp(s_ref[h, part, :] - tops[h])
            total = total + jnp.sum(e, 0, keepdims=True)
            e = e.astype(bf16)
            e_ref[h, part, :] = e
            acc = acc + jnp.dot(
                values_t[h * hd : (h + 1) * hd, :], e, preferred_element_type=f32
            )
            out.append((total, acc))
        return tuple(out)

    mixed = lax.fori_loop(
        0,
        used,
        mix,
        tuple((jnp.zeros((1, rows), f32), jnp.zeros((hd, rows), f32)) for _ in range(heads)),
    )
    ctx_parts, dcn_parts, deltas = [], [], []
    for h in range(heads):
        total, acc = mixed[h]
        inv = 1.0 / total
        ctx_h = acc * inv
        dc_h = dc_t[h * hd : (h + 1) * hd, :]
        deltas.append(jnp.sum(ctx_h * dc_h, 0, keepdims=True) * inv)
        ctx_parts.append(ctx_h)
        dcn_parts.append(dc_h * inv)
    y_ref[here, :width] = jnp.concatenate(ctx_parts, 0).T.astype(bf16)
    dcn_t = jnp.concatenate(dcn_parts, 0)
    dcn = dcn_t.T
    dcn_heads_t = [jnp.where(row_head == h, dcn_t, 0.0).astype(bf16) for h in range(heads)]
    dcn_heads = [jnp.where(lane_head == h, dcn, 0.0).astype(bf16) for h in range(heads)]

    def back(j, carry):
        part = pl.ds(pl.multiple_of(j * chunk, chunk), chunk)
        values = v_ref[part, :]
        keys_t = kt_ref[j]
        dk = dk_acc[part, :]
        dv = dv_acc[part, :]
        out = []
        for h in range(heads):
            e = e_ref[h, part, :]
            dp = jnp.dot(values, dcn_heads_t[h], preferred_element_type=f32)
            ds = (e.astype(f32) * (dp - deltas[h])).astype(bf16)
            out.append(
                carry[h]
                + jnp.dot(keys_t[h * hd : (h + 1) * hd, :], ds, preferred_element_type=f32)
            )
            dk = dk + jnp.dot(ds, q_heads[h], preferred_element_type=f32)
            dv = dv + jnp.dot(e, dcn_heads[h], preferred_element_type=f32)
        dk_acc[part, :] = dk
        dv_acc[part, :] = dv
        return tuple(out)

    dq = lax.fori_loop(
        0, used, back, tuple(jnp.zeros((hd, rows), f32) for _ in range(heads))
    )
    y_ref[here, width : 2 * width] = (jnp.concatenate(dq, 0).T * HD ** (-0.5)).astype(bf16)

    @pl.when(step == pl.num_programs(0) - 1)
    def _():
        y_ref[:, 2 * width : 3 * width] = dk_acc[...].astype(bf16)
        y_ref[:, 3 * width :] = dv_acc[...].astype(bf16)
        for flip in range(flips):
            outs[flip][...] = y_ref[spot(flip), :]


def attention(blocks, seg, place, block=256, chunk=256):
    flips = len(blocks) // 2
    span, width = blocks[-1].shape
    count, columns = span * flips, 4 * width
    heads = width // HD
    bf16 = jnp.bfloat16
    f32 = jnp.float32
    pairs = count * (count + block) // 2 * heads
    whole = pl.BlockSpec((span, columns), lambda i, p: (0, 0))
    return pl.pallas_call(
        lambda *refs: attention_body(heads, flips, *refs),
        grid_spec=pltpu.PrefetchScalarGridSpec(
            num_scalar_prefetch=1,
            grid=(count // block,),
            in_specs=[pl.BlockSpec(block.shape, lambda i, p: (0, 0)) for block in blocks]
            + [
                pl.BlockSpec((count, 1), lambda i, p: (0, 0)),
                pl.BlockSpec((1, block), lambda i, p: (0, i)),
            ],
            out_specs=[whole] * flips,
            scratch_shapes=[
                pltpu.VMEM((count, columns), bf16),
                pltpu.VMEM((count, columns), bf16),
                pltpu.VMEM((count // chunk, width, chunk), bf16),
                pltpu.VMEM((count // chunk, width, chunk), bf16),
                pltpu.VMEM((heads, count, block), f32),
                pltpu.VMEM((heads, count, block), bf16),
                pltpu.VMEM((count, width), f32),
                pltpu.VMEM((count, width), f32),
            ],
        ),
        out_shape=[jax.ShapeDtypeStruct((span, columns), bf16)] * flips,
        compiler_params=pltpu.CompilerParams(vmem_limit_bytes=48 * 1024 * 1024),
        cost_estimate=pl.CostEstimate(
            flops=10 * pairs * HD * 3, bytes_accessed=count * width * 16, transcendentals=pairs
        ),
        name="attention",
    )(place.reshape(1), *blocks, seg[:, None], seg[None, :])


def norm_rows(x, slot, params_ref, outs):
    bf16 = jnp.bfloat16
    first_ref, second_ref, normed_ref = outs
    normed, _ = normalize(x.astype(jnp.float32))
    normed_ref[0, slot] = normed.astype(bf16)
    first_ref[0, slot] = (normed * params_ref[0:1] + params_ref[1:2]).astype(bf16)
    second_ref[0, slot] = (normed * params_ref[2:3] + params_ref[3:4]).astype(bf16)


def merge_rows(x, slot, params_ref, outs):
    outs[0][0, slot] = x


def both_cores(rows_body, own, mine, other, core, params, results):
    size = len(mine) + 1
    half, cols = mine[0].shape

    def run(core_ref, *refs):
        own_ref, refs = refs[0], refs[1:]
        ins, params_ref, outs = refs[: 2 * size - 2], refs[2 * size - 2], refs[2 * size - 1 :]
        core = core_ref[0]

        @pl.when(pl.program_id(0) == 0)
        def _():
            for slot in range(2):
                rows_body(own_ref[slot * half : (slot + 1) * half, :], slot, params_ref, outs)

        for chip in range(1, size):

            @pl.when(pl.program_id(0) == chip)
            def _(chip=chip):
                rows_body(ins[chip - 1][...], core, params_ref, outs)
                rows_body(ins[size + chip - 2][...], 1 - core, params_ref, outs)

    made = pl.pallas_call(
        run,
        grid_spec=pltpu.PrefetchScalarGridSpec(
            num_scalar_prefetch=1,
            grid=(size,),
            in_specs=[pl.BlockSpec(own.shape, lambda i, c: (0, 0))]
            + [pl.BlockSpec((half, cols), lambda i, c: (0, 0))] * (2 * size - 2)
            + [pl.BlockSpec(params.shape, lambda i, c: (0, 0))],
            out_specs=[pl.BlockSpec((1, 2, half, cols), lambda i, c: (i, 0, 0, 0))] * results,
        ),
        out_shape=[jax.ShapeDtypeStruct((size, 2, half, cols), own.dtype)] * results,
        compiler_params=pltpu.CompilerParams(vmem_limit_bytes=32 * 1024 * 1024),
        cost_estimate=pl.CostEstimate(
            flops=size * half * cols * 20,
            bytes_accessed=size * half * cols * 4 * (1 + results),
            transcendentals=0,
        ),
        name=rows_body.__name__,
    )(core.reshape(1), own, *mine, *other, params)
    return [x.reshape(size * 2 * half, cols) for x in made]


def partner(tensor, axis, flip):
    size = lax.axis_size(axis)
    return lax.ppermute(tensor, axis, [(s, s ^ flip) for s in range(size)])


def pick(tensor, index, size, dim=0):
    return lax.dynamic_slice_in_dim(tensor, index * size, size, dim)


def swap(tensor, axis):
    return lax.all_to_all(tensor, axis, 0, 0)


def gather(block, axis):
    return swap(jnp.broadcast_to(block[None], (lax.axis_size(axis),) + block.shape), axis)


def chip_start(partial, size):
    f32 = jnp.float32
    core = lax.axis_index("tp")
    halves = partial.reshape(size, 2, -1, partial.shape[1])
    away = lax.dynamic_index_in_dim(halves, 1 - core, 1, keepdims=False)
    kept = lax.dynamic_index_in_dim(halves, core, 1, keepdims=False)
    return (kept.astype(f32) + partner(away, "tp", 1).astype(f32)).astype(partial.dtype)


def chip_join(mine, other):
    core = lax.axis_index("tp")
    low = jnp.where(core == 0, mine, other)
    high = jnp.where(core == 0, other, mine)
    return jnp.concatenate([low, high], 0)


def pack_wide(up, down, out, chips, part):
    span = down.shape[2] // chips
    for chip in range(chips):
        out[0, chip, :part, :] = up[chip, 0]
        for half in range(2):
            out[0, chip, part:, half * span : (half + 1) * span] = down[
                0, half * part : (half + 1) * part, chip * span : (chip + 1) * span
            ]


def pack_heads(joint, outw, out, low, chips, part):
    width = joint.shape[4]
    span = outw.shape[3] // chips // 2
    rows = part // 2
    for chip in range(chips):
        out[0, chip, :, :width] = joint[chip, 0, low]
        for half in range(2):
            begin = (2 * chip + half) * span
            out[0, chip, half * rows : (half + 1) * rows, width:] = outw[
                0, low, :, begin : begin + span
            ]


def unpack_wide(x, up, down, chips, part):
    f32 = jnp.float32
    span = down.shape[3]
    cols = x.shape[2]
    for chip in range(chips):
        up[:, chip * cols : (chip + 1) * cols] = x[chip, :part, :].astype(f32)
        for half in range(2):
            down[chip, 0, half * part : (half + 1) * part, :] = x[
                chip, part:, half * span : (half + 1) * span
            ].astype(f32)


def unpack_heads(x, joint, outw, chips, part):
    f32 = jnp.float32
    span = outw.shape[3] // 2
    rows = part // 2
    width = joint.shape[2] // chips
    for chip in range(chips):
        for kind in range(3):
            joint[kind, :, chip * width : (chip + 1) * width] = x[
                chip, :, kind * width : (kind + 1) * width
            ].astype(f32)
        for half in range(2):
            outw[chip, 0, :, half * span : (half + 1) * span] = x[
                chip, half * rows : (half + 1) * rows, 3 * width :
            ].astype(f32)


def unpack(body, blocks, wide, wide_block, tall, tall_block, place):
    f32 = jnp.float32
    chips, rows, cols = blocks[0].shape
    depth = len(blocks)
    whole = pl.BlockSpec((chips, rows, cols), lambda i, p: (0, 0, 0))

    def run(place_ref, *refs):
        for k in range(depth):

            @pl.when(pl.program_id(0) == k)
            def _(k=k):
                body(refs[k], refs[depth], refs[depth + 1], chips, cols // 8)

    def at(dim, count):
        return lambda i, p: tuple((p[0] ^ i) if d == dim else 0 for d in range(count))

    dim = len(wide) - 2
    return pl.pallas_call(
        run,
        grid_spec=pltpu.PrefetchScalarGridSpec(
            num_scalar_prefetch=1,
            grid=(depth,),
            in_specs=[whole] * depth,
            out_specs=[
                pl.BlockSpec(wide_block, at(dim, len(wide))),
                pl.BlockSpec(tall_block, at(1, len(tall))),
            ],
        ),
        out_shape=[jax.ShapeDtypeStruct(wide, f32), jax.ShapeDtypeStruct(tall, f32)],
        compiler_params=pltpu.CompilerParams(vmem_limit_bytes=24 * 1024 * 1024),
        cost_estimate=pl.CostEstimate(
            flops=0, bytes_accessed=6 * depth * chips * rows * cols, transcendentals=0
        ),
        name=body.__name__,
    )(place.reshape(1), *blocks)


def pack_slots(body, wide, tall, rows, chips, place):
    depth = 4
    part = wide.shape[0] // chips // depth
    cols = part * 8
    wide = wide.reshape(chips, 1, depth, part, wide.shape[1])
    tall = tall.reshape(1, depth, tall.shape[0] // depth, tall.shape[1])

    def run(place_ref, wide_ref, tall_ref, *outs):
        for k in range(depth):
            body(wide_ref, tall_ref, outs[k], place_ref[0] ^ k, chips, part)

    return pl.pallas_call(
        run,
        grid_spec=pltpu.PrefetchScalarGridSpec(
            num_scalar_prefetch=1,
            grid=(1,),
            in_specs=[
                pl.BlockSpec(wide.shape, lambda i, p: (0, 0, 0, 0, 0)),
                pl.BlockSpec(tall.shape, lambda i, p: (0, 0, 0, 0)),
            ],
            out_specs=[pl.BlockSpec((1, chips, rows, cols), lambda i, p: (0, 0, 0, 0))] * depth,
        ),
        out_shape=[jax.ShapeDtypeStruct((1, chips, rows, cols), jnp.bfloat16)] * depth,
        compiler_params=pltpu.CompilerParams(vmem_limit_bytes=24 * 1024 * 1024),
        cost_estimate=pl.CostEstimate(
            flops=0, bytes_accessed=16 * chips * rows * cols, transcendentals=0
        ),
        name=body.__name__,
    )(place.reshape(1), wide, tall)


def pack_all(body, wide, tall, rows, chips):
    depth = 4
    part = wide.shape[0] // chips // depth
    cols = part * 8
    wide = wide.reshape(chips, depth, part, wide.shape[1])
    tall = tall.reshape(depth, tall.shape[0] // depth, tall.shape[1])

    def run(wide_ref, tall_ref, out):
        body(wide_ref, tall_ref, out, chips, part)

    return pl.pallas_call(
        run,
        grid=(depth,),
        in_specs=[
            pl.BlockSpec((chips, 1, part, wide.shape[3]), lambda i: (0, i, 0, 0)),
            pl.BlockSpec((1,) + tall.shape[1:], lambda i: (i, 0, 0)),
        ],
        out_specs=pl.BlockSpec((1, chips, rows, cols), lambda i: (i, 0, 0, 0)),
        out_shape=jax.ShapeDtypeStruct((depth, chips, rows, cols), jnp.bfloat16),
        compiler_params=pltpu.CompilerParams(vmem_limit_bytes=24 * 1024 * 1024),
        cost_estimate=pl.CostEstimate(
            flops=0, bytes_accessed=4 * depth * chips * rows * cols, transcendentals=0
        ),
        name="pack_wide",
    )(wide, tall)


def add_slots(slots):
    total = slots[0][0].astype(jnp.float32)
    for slot in slots[1:]:
        total = total + slot[0].astype(jnp.float32)
    return total.astype(jnp.bfloat16)


def send_slots(slots):
    return [slots[0]] + [partner(slots[k], "ctx", k) for k in range(1, len(slots))]


def after(tensor, *others):
    return lax.optimization_barrier((tensor,) + others)[0]


def hidden_body(second_ref, cot_ref, up_ref, down_ref, bias_ref, act_ref, dup_ref, sum_ref):
    f32 = jnp.float32
    bf16 = jnp.bfloat16
    upper = jnp.dot(second_ref[...], up_ref[...], preferred_element_type=f32)
    upper = upper + bias_ref[...]
    share = 0.5 + 0.5 * lax.erf(upper * 0.5**0.5)
    act_ref[...] = (upper * share).astype(bf16)
    d_act = lax.dot_general(
        cot_ref[...], down_ref[...], (((1,), (1,)), ((), ())), preferred_element_type=f32
    )
    bell = jnp.exp(-0.5 * upper * upper) * (0.5 / jnp.pi) ** 0.5
    d_upper = d_act * (share + upper * bell)
    dup_ref[...] = d_upper.astype(bf16)

    @pl.when(pl.program_id(0) == 0)
    def _():
        sum_ref[...] = jnp.zeros_like(sum_ref)

    sum_ref[...] += jnp.sum(d_upper, 0, keepdims=True)


def hidden_layer(second, cot_b, up_w, down_w, up_bias, block=256):
    f32 = jnp.float32
    bf16 = jnp.bfloat16
    count, model = second.shape
    hidden = up_w.shape[1]
    rows = pl.BlockSpec((block, model), lambda i: (i, 0))
    made = pl.BlockSpec((block, hidden), lambda i: (i, 0))
    act, dup, total = pl.pallas_call(
        hidden_body,
        grid=(count // block,),
        in_specs=[
            rows,
            rows,
            pl.BlockSpec((model, hidden), lambda i: (0, 0)),
            pl.BlockSpec((hidden, model), lambda i: (0, 0)),
            pl.BlockSpec((1, hidden), lambda i: (0, 0)),
        ],
        out_specs=[made, made, pl.BlockSpec((1, hidden), lambda i: (0, 0))],
        out_shape=[
            jax.ShapeDtypeStruct((count, hidden), bf16),
            jax.ShapeDtypeStruct((count, hidden), bf16),
            jax.ShapeDtypeStruct((1, hidden), f32),
        ],
        compiler_params=pltpu.CompilerParams(vmem_limit_bytes=32 * 1024 * 1024),
        cost_estimate=pl.CostEstimate(
            flops=4 * count * model * hidden,
            bytes_accessed=4 * count * (model + hidden) + 4 * model * hidden,
            transcendentals=2 * count * hidden,
        ),
        name="hidden_layer",
    )(second, cot_b, up_w, down_w, up_bias.astype(f32)[None])
    return act, dup, total[0]


def plane_local(
    tokens,
    segment_ids,
    positions,
    attention_gain,
    attention_shift,
    feedforward_gain,
    feedforward_shift,
    joint_weight,
    joint_bias,
    output_weight,
    output_bias,
    up_weight,
    up_bias,
    down_weight,
    down_bias,
    cotangent,
):
    f32 = jnp.float32
    bf16 = jnp.bfloat16
    me, place, core = lax.axis_index("fsdp"), lax.axis_index("ctx"), lax.axis_index("tp")
    size = lax.axis_size("fsdp")
    depth = lax.axis_size("ctx")
    count, model = tokens.shape[1:]
    half_rows = count // 2
    rows = tokens[0].astype(f32)
    cot = cotangent[0]

    half = pick(tokens[0], core, half_rows)
    my_tokens = [partner(half, "fsdp", k) for k in range(1, size)]
    cot_half, _ = lax.optimization_barrier((cot.astype(bf16), tuple(my_tokens)))
    half = pick(cot_half, core, half_rows)
    my_cot = [partner(half, "fsdp", k) for k in range(1, size)]
    width = joint_weight.shape[2] // size
    small = jnp.concatenate(
        [
            attention_gain,
            attention_shift,
            feedforward_gain,
            feedforward_shift,
            output_bias,
            down_bias,
        ]
    ).astype(f32)
    notes = jnp.concatenate([small, segment_ids[0].astype(f32), positions[0].astype(f32)])
    packed = gather(
        notes,
        ("fsdp", "ctx"),
    ).reshape(size, depth, -1)
    joint_send = joint_weight.reshape(-1, 3, size, width).transpose(2, 0, 1, 3)
    tokens_other = [partner(block, "tp", 1) for block in my_tokens]
    joint_w = swap(after(joint_send, packed), "fsdp")
    joint_w = after(joint_w, *tokens_other).reshape(model, 3, width)
    params = packed[:, 0, : small.size].reshape(size, 6, -1).transpose(1, 0, 2).reshape(6, model)
    seg_seq = lax.dynamic_index_in_dim(packed, place, 0, keepdims=False)
    seg_seq = seg_seq[:, small.size : small.size + count].reshape(-1)
    pos_here = lax.dynamic_index_in_dim(packed, place, 1, keepdims=False)[:, small.size + count :]
    pos_plane = jnp.concatenate(
        [lax.dynamic_index_in_dim(pos_here, me ^ k, 0, keepdims=False) for k in range(size)]
    )
    first, second, normed = both_cores(
        norm_rows, tokens[0], my_tokens, tokens_other, core, params[:4], 3
    )
    output_w = swap(after(output_weight, first).reshape(size, width, -1), "fsdp")
    output_w = output_w.transpose(1, 0, 2).reshape(width, model)
    cot_other = [partner(block, "tp", 1) for block in my_cot]
    (cot_b,) = both_cores(merge_rows, cot_half, my_cot, cot_other, core, params[:4], 1)
    hidden = up_weight.shape[1] // size
    up_send = up_weight.reshape(-1, size, hidden).transpose(1, 0, 2)
    up_w = swap(after(up_send, output_w, first, cot_b), "fsdp")
    up_w = up_w.reshape(model, hidden)
    down_w = swap(after(down_weight, up_w).reshape(size, hidden, -1), "fsdp")
    down_w = down_w.transpose(1, 0, 2).reshape(hidden, model)


    lane = jnp.arange(width, dtype=jnp.int32) % HD
    half = ROT // 2
    freq = jnp.where(
        lane < ROT, ROPE_BASE ** (-((lane % half).astype(f32) * 2.0 / ROT)), 0.0
    )
    angle = pos_plane[:, None] * freq[None, :]
    cosine = jnp.cos(angle)
    sine = jnp.sin(angle) * jnp.where(lane < half, -1.0, 1.0)[None, :]
    source = jnp.arange(width, dtype=jnp.int32)
    source = jnp.where(lane < half, source + half, jnp.where(lane < ROT, source - half, -1))
    turn = (jnp.arange(width, dtype=jnp.int32)[:, None] == source[None, :]).astype(bf16)

    joint_flat = joint_w.reshape(model, 3 * width)
    bias = joint_bias.astype(f32)
    joint = jnp.dot(first, joint_flat, preferred_element_type=f32) + bias.reshape(-1)[None]
    swapped_w = jnp.einsum("dpe,ef->dpf", joint_w[:, :2], turn, preferred_element_type=bf16)
    swapped_b = jnp.dot(joint_bias[:2], turn, preferred_element_type=f32)
    swapped = (
        jnp.dot(first, swapped_w.reshape(model, 2 * width), preferred_element_type=f32)
        + swapped_b.reshape(-1)[None]
    )
    scale = HD ** (-0.5)
    queries = (joint[:, :width] * cosine + swapped[:, :width] * sine) * scale
    keys = joint[:, width : 2 * width] * cosine + swapped[:, width:] * sine
    d_context = jnp.einsum("nd,wd->nw", cot_b, output_w, preferred_element_type=f32)
    sending = jnp.concatenate([queries, keys, joint[:, 2 * width :]], 1).astype(bf16)
    blocks = []
    for tensor in (sending, d_context.astype(bf16)):
        for flip in range(depth):
            block = pick(tensor, me ^ place ^ flip, count)
            blocks.append(partner(block, "ctx", flip) if flip else block)
    second, up_w = lax.optimization_barrier((second, up_w, sending))[:2]

    activated, d_upper_b, grad_up_b = hidden_layer(second, cot_b, up_w, down_w, up_bias)
    moment_up = jnp.dot(normed.T, d_upper_b, preferred_element_type=f32)
    d_upper_sum = jnp.sum(d_upper_b.astype(f32), 0)
    grad_up_w = (
        params[2][:, None] * moment_up + params[3][:, None] * d_upper_sum[None, :]
    ).astype(bf16)
    up_f32 = up_w.astype(f32)
    gain_two_grad = jnp.sum(up_f32 * moment_up, 1)
    shift_two_grad = jnp.sum(up_f32 * d_upper_sum[None, :], 1)
    grad_down_w = jnp.dot(activated.T, cot_b, preferred_element_type=f32).astype(bf16)
    part = model // size // depth
    packed_wide = pack_all(pack_wide, grad_up_w, grad_down_w, 2 * part, size)
    blocks, packed_wide = lax.optimization_barrier((tuple(blocks), packed_wide))
    made = attention(blocks, seg_seq, place)
    made, packed_wide = lax.optimization_barrier((tuple(made), swap(packed_wide, "ctx")))
    held_wide = swap(jnp.sum(packed_wide.astype(f32), 0).astype(bf16), "fsdp")
    gained = (up_f32 * params[2][:, None]).astype(bf16)
    upstream_two = jnp.einsum("nf,df->nd", d_upper_b, gained, preferred_element_type=f32)
    upstream_two = upstream_two.astype(bf16)
    mixed_two = jnp.dot(activated, down_w, preferred_element_type=f32).astype(bf16)

    back = jnp.zeros((size * count, 4 * width), bf16)
    made = [made[0]] + [partner(made[k], "ctx", k) for k in range(1, depth)]
    made, held_wide = lax.optimization_barrier((tuple(made), held_wide))
    near_far = partner(held_wide, "ctx", 1), partner(held_wide, "ctx", 2)
    for flip in range(depth):
        block = made[flip]
        back = lax.dynamic_update_slice_in_dim(back, block, (me ^ place ^ flip) * count, 0)
    context = back[:, :width]
    d_qk = back[:, width : 3 * width]

    d_swapped = jnp.einsum(
        "npe,ef->npf", d_qk.reshape(-1, 2, width), turn, preferred_element_type=f32
    ).reshape(-1, 2 * width)
    cosines = jnp.concatenate([cosine, cosine], 1)
    sines = jnp.concatenate([sine, sine], 1)
    d_joint = jnp.concatenate(
        [d_qk.astype(f32) * cosines - d_swapped * sines, back[:, 3 * width :].astype(f32)], 1
    )
    d_joint_b = d_joint.astype(bf16)
    joint_f32 = joint_flat.astype(f32)
    gained = (joint_f32 * params[0][:, None]).astype(bf16)
    mixed = jnp.dot(context, output_w, preferred_element_type=f32) + mixed_two.astype(f32)
    mixed = mixed.astype(bf16)
    upstream = jnp.einsum("ne,de->nd", d_joint_b, gained, preferred_element_type=f32)
    upstream = (upstream + upstream_two.astype(f32)).astype(bf16)
    d_joint_b, context = lax.optimization_barrier((d_joint_b, context, mixed, upstream))[:2]
    sending_result = chip_start(mixed, size)
    sending_up = chip_start(upstream, size)
    got_result = partner(sending_result[2:], "fsdp", 2)
    got_up = partner(sending_up[1::2], "fsdp", 1)
    grad_joint_b = jnp.sum(d_joint, 0)
    moment_joint = jnp.dot(normed.T, d_joint_b, preferred_element_type=f32)
    d_joint_sum = jnp.sum(d_joint_b.astype(f32), 0)
    grad_joint_w = (
        params[0][:, None] * moment_joint + params[1][:, None] * d_joint_sum[None, :]
    ).astype(bf16)
    grad_output_w = jnp.dot(context.T, cot_b, preferred_element_type=f32).astype(bf16)
    slots = pack_slots(pack_heads, grad_joint_w, grad_output_w, part, size, place)
    slots = send_slots(slots)
    stats = jnp.stack(
        [
            jnp.sum(joint_f32 * moment_joint, 1),
            jnp.sum(joint_f32 * d_joint_sum[None, :], 1),
            gain_two_grad,
            shift_two_grad,
            jnp.sum(pick(cot, core, half_rows), 0),
        ]
    )
    stats = stats.reshape(5, size, 1, -1).transpose(1, 2, 0, 3).reshape(size, 1, -1)
    biases = jnp.concatenate([grad_joint_b, grad_up_b])
    biases = jnp.broadcast_to(biases[None, None], (size, 1, 3 * width + hidden))
    stats_size = stats.shape[2]
    packed = jnp.concatenate([stats, biases], 2)
    packed = jnp.broadcast_to(packed, (size, 2 * depth, packed.shape[2]))
    packed = swap(packed.reshape(2 * size * depth, 1, -1), ("fsdp", "ctx", "tp"))
    got_result, got_up = lax.optimization_barrier((got_result, got_up))
    half_result = sending_result[:2].astype(f32) + got_result.astype(f32)
    half_up = sending_up[::2].astype(f32) + got_up.astype(f32)
    got_result = partner(half_result[1].astype(bf16), "fsdp", 1)
    got_up = partner(half_up[1].astype(bf16), "fsdp", 2)
    slots, near_far, got_result, got_up, packed = lax.optimization_barrier(
        (tuple(slots), near_far, got_result, got_up, packed)
    )

    held = swap(add_slots(slots), "fsdp")
    last = partner(near_far[1], "ctx", 1)
    my_rows = pick(rows, core, half_rows)
    result = my_rows + half_result[0] + got_result.astype(f32) + params[4] + params[5]
    normed_here, rstd = normalize(my_rows)
    upstream = half_up[0] + got_up.astype(f32)
    tokens_grad = pick(cot, core, half_rows) + rstd * (
        upstream
        - jnp.mean(upstream, -1, keepdims=True)
        - normed_here * jnp.mean(upstream * normed_here, -1, keepdims=True)
    )
    other_result = partner(result, "tp", 1)
    other_grad = partner(tokens_grad, "tp", 1)
    held, last, other_result, other_grad = lax.optimization_barrier(
        (held, last, other_result, other_grad)
    )

    slots = send_slots([held[None]] * depth)
    result = chip_join(result, other_result)
    tokens_grad = chip_join(tokens_grad, other_grad)
    packed = packed.reshape(size, depth, 2, -1)
    owned = jnp.sum(packed[..., :stats_size], (0, 1, 2)).reshape(5, -1)
    biases = lax.dynamic_index_in_dim(packed[..., stats_size:], me, 0, keepdims=False)
    biases = jnp.sum(lax.dynamic_index_in_dim(biases, core, 1, keepdims=False), 0)
    owned_jbias = biases[: 3 * width].reshape(3, width)
    owned_upbias = biases[3 * width :]
    owned_up, owned_down = unpack(
        unpack_wide,
        (held_wide, near_far[0], near_far[1], last),
        (model // size, up_weight.shape[1]),
        (part, up_weight.shape[1]),
        (size, depth, 2 * part, 2 * width),
        (size, 1, 2 * part, 2 * width),
        place,
    )
    owned_down = owned_down.reshape(down_weight.shape)
    owned_joint, owned_output = unpack(
        unpack_heads,
        [slot[0] for slot in slots],
        (3, model // size, joint_weight.shape[2]),
        (3, part, joint_weight.shape[2]),
        (size, depth, part // 2, 2 * width),
        (size, 1, part // 2, 2 * width),
        place,
    )
    owned_joint = owned_joint.transpose(1, 0, 2)
    owned_output = owned_output.reshape(output_weight.shape)
    return (
        result[None],
        tokens_grad[None],
        owned[0],
        owned[1],
        owned[2],
        owned[3],
        owned_joint,
        owned_jbias,
        owned_output,
        owned[4],
        owned_up,
        owned_upbias,
        owned_down,
        owned[4],
    )


def splits_plane(mesh, tokens, joint_weight, up_weight):
    size, depth, cores = mesh.shape["fsdp"], mesh.shape["ctx"], mesh.shape["tp"]
    width = joint_weight.shape[2] // (size * cores)
    return (
        size == depth == tokens.shape[0] == 4
        and cores == 2
        and width % 128 == 0
        and tokens.shape[2] == 2 * size * width
        and up_weight.shape[1] == 4 * size * cores * width
        and tokens.shape[1] // depth % 256 == 0
    )


def solution(mesh):
    placed = (
        P("fsdp", "ctx", None),
        P("fsdp", "ctx"),
        P("fsdp", "ctx"),
        P("fsdp"),
        P("fsdp"),
        P("fsdp"),
        P("fsdp"),
        P("fsdp", None, "tp"),
        P(None, ("tp", "fsdp")),
        P("tp", "fsdp"),
        P("fsdp"),
        P("fsdp", "tp"),
        P(("tp", "fsdp")),
        P("tp", "fsdp"),
        P("fsdp"),
        P("fsdp", "ctx", None),
    )
    given = (
        P("fsdp", "ctx", None),
        P("fsdp", "ctx", None),
        P("fsdp"),
        P("fsdp"),
        P("fsdp"),
        P("fsdp"),
        P("fsdp", None, "tp"),
        P(None, ("tp", "fsdp")),
        P("tp", "fsdp"),
        P("fsdp"),
        P("fsdp", "tp"),
        P(("tp", "fsdp")),
        P("tp", "fsdp"),
        P("fsdp"),
    )

    def run(*args):
        body = plane_local if splits_plane(mesh, args[0], args[7], args[11]) else gathered_local
        return jax.shard_map(
            body, mesh=mesh, in_specs=placed, out_specs=given, check_vma=False
        )(*args)

    return run
```

```python
import jax
import jax.numpy as jnp
from jax import lax
from jax.experimental import pallas as pl
from jax.experimental.pallas import tpu as pltpu
from jax.sharding import PartitionSpec as P

HD = 64
ROT = 16


EPS = 1e-05
ROPE_BASE = 10000.0


def rope_tables(offsets):
    half_dim = ROT // 2
    freq = ROPE_BASE ** (-(jnp.arange(half_dim, dtype=jnp.float32) * 2.0 / ROT))
    angle = offsets.astype(jnp.float32)[:, None] * freq[None, :]
    return (jnp.cos(angle)[:, None, :], jnp.sin(angle)[:, None, :])


def rotate(tensor, cosine, sine):
    half_dim = ROT // 2
    front = tensor[..., :half_dim]
    middle = tensor[..., half_dim:ROT]
    return jnp.concatenate(
        [front * cosine - middle * sine, middle * cosine + front * sine, tensor[..., ROT:]], axis=-1
    )


def unrotate(grads, cosine, sine):
    half_dim = ROT // 2
    front = grads[..., :half_dim]
    middle = grads[..., half_dim:ROT]
    return jnp.concatenate(
        [front * cosine + middle * sine, middle * cosine - front * sine, grads[..., ROT:]], axis=-1
    )


def normalize(rows):
    center = jnp.mean(rows, -1, keepdims=True)
    centred = rows - center
    spread = jnp.mean(centred * centred, -1, keepdims=True)
    rstd = lax.rsqrt(spread + EPS)
    return (centred * rstd, rstd)


def norm_back(upstream, normed, rstd, gain):
    scaled = upstream * gain
    return rstd * (
        scaled
        - jnp.mean(scaled, -1, keepdims=True)
        - normed * jnp.mean(scaled * normed, -1, keepdims=True)
    )


def masked_scores(query_blk, query_index, query_seg, keys, key_seg):
    scores = jnp.einsum(
        "qhe,khe->hqk", query_blk, keys, preferred_element_type=jnp.float32
    ) * HD ** (-0.5)
    key_index = jnp.arange(keys.shape[0], dtype=jnp.int32)
    allowed = (key_seg[None, :] == query_seg[:, None]) & (
        key_index[None, :] <= query_index[:, None]
    )
    return jnp.where(allowed[None], scores, -jnp.inf)


def gathered_local(
    tokens,
    segment_ids,
    positions,
    attention_gain,
    attention_shift,
    feedforward_gain,
    feedforward_shift,
    joint_weight,
    joint_bias,
    output_weight,
    output_bias,
    up_weight,
    up_bias,
    down_weight,
    down_bias,
    cotangent,
):
    f32 = jnp.float32
    bf16 = jnp.bfloat16
    scale = HD ** (-0.5)
    small = jnp.stack(
        [
            attention_gain,
            attention_shift,
            feedforward_gain,
            feedforward_shift,
            output_bias,
            down_bias,
        ]
    )
    full_joint, full_output, full_up, full_down, full_small, full_jbias, full_upbias = (
        lax.all_gather(joint_weight, "fsdp", axis=0, tiled=True),
        lax.all_gather(output_weight, "fsdp", axis=1, tiled=True),
        lax.all_gather(up_weight, "fsdp", axis=0, tiled=True),
        lax.all_gather(down_weight, "fsdp", axis=1, tiled=True),
        lax.all_gather(small, "fsdp", axis=1, tiled=True),
        lax.all_gather(joint_bias, "fsdp", axis=1, tiled=True),
        lax.all_gather(up_bias, "fsdp", axis=0, tiled=True),
    )
    params = full_small.astype(f32)
    gain_one = params[0]
    shift_one = params[1]
    gain_two = params[2]
    shift_two = params[3]
    rows = tokens[0].astype(f32)
    count_rows = rows.shape[0]
    local_width = joint_weight.shape[2]
    heads_here = local_width // HD
    normed, rstd = normalize(rows)
    first = (normed * gain_one + shift_one).astype(bf16)
    second = (normed * gain_two + shift_two).astype(bf16)
    joint = (
        jnp.einsum("nd,dpe->npe", first, full_joint, preferred_element_type=f32)
        + full_jbias.astype(f32)[None]
    )
    cosine, sine = rope_tables(positions[0])
    queries = rotate(joint[:, 0].reshape(count_rows, heads_here, HD), cosine, sine).astype(bf16)
    keys_here = rotate(joint[:, 1].reshape(count_rows, heads_here, HD), cosine, sine).astype(bf16)
    values_here = joint[:, 2].reshape(count_rows, heads_here, HD).astype(bf16)
    seg_here = segment_ids[0]
    all_keys, all_values, all_segs = (
        lax.all_gather(keys_here, "ctx", axis=0, tiled=True),
        lax.all_gather(values_here, "ctx", axis=0, tiled=True),
        lax.all_gather(seg_here.astype(bf16), "ctx", axis=0, tiled=True),
    )
    key_seg = all_segs.astype(f32)
    query_seg = seg_here.astype(f32)
    query_index = lax.axis_index("ctx") * count_rows + jnp.arange(count_rows, dtype=jnp.int32)
    block = min(512, count_rows)
    count_blocks = count_rows // block
    query_blocks = queries.reshape(count_blocks, block, heads_here, HD)
    index_blocks = query_index.reshape(count_blocks, block)
    seg_blocks = query_seg.reshape(count_blocks, block)

    def forward_block(args):
        query_blk, block_index, block_seg = args
        scores = masked_scores(query_blk, block_index, block_seg, all_keys, key_seg)
        top = jnp.max(scores, -1, keepdims=True)
        lse = top + jnp.log(jnp.sum(jnp.exp(scores - top), -1, keepdims=True))
        probs = jnp.exp(scores - lse).astype(bf16)
        mixed = jnp.einsum("hqk,khe->qhe", probs, all_values, preferred_element_type=f32)
        return (mixed, lse[..., 0])

    context32, lse_all = lax.map(forward_block, (query_blocks, index_blocks, seg_blocks))
    context32 = context32.reshape(count_rows, local_width)
    context = context32.astype(bf16)
    upper = jnp.dot(second, full_up, preferred_element_type=f32) + full_upbias.astype(f32)
    activated = jax.nn.gelu(upper, approximate=False).astype(bf16)
    partial_value = jnp.dot(context, full_output, preferred_element_type=f32) + jnp.dot(
        activated, full_down, preferred_element_type=f32
    )
    mixed_all = lax.psum(partial_value, "tp")
    result = rows + mixed_all + params[4] + params[5]
    back_joint, back_output, back_up, back_down = (
        lax.all_gather(joint_weight, "fsdp", axis=0, tiled=True),
        lax.all_gather(output_weight, "fsdp", axis=1, tiled=True),
        lax.all_gather(up_weight, "fsdp", axis=0, tiled=True),
        lax.all_gather(down_weight, "fsdp", axis=1, tiled=True),
    )
    cot = cotangent[0]
    cot_b = cot.astype(bf16)
    grad_output_w = jnp.dot(context.T, cot_b, preferred_element_type=f32)
    bias_sum = jnp.sum(cot, 0)
    grad_down_w = jnp.dot(activated.T, cot_b, preferred_element_type=f32)
    d_act = jnp.einsum("nd,fd->nf", cot_b, back_down, preferred_element_type=f32)
    unused, gelu_back = jax.vjp(lambda value: jax.nn.gelu(value, approximate=False), upper)
    d_upper = gelu_back(d_act)[0]
    d_upper_b = d_upper.astype(bf16)
    grad_up_w = jnp.dot(second.T, d_upper_b, preferred_element_type=f32)
    grad_up_b = jnp.sum(d_upper, 0)
    d_second_part = jnp.einsum("nf,df->nd", d_upper_b, back_up, preferred_element_type=f32)
    d_context = (
        jnp.einsum("nd,wd->nw", cot_b, back_output, preferred_element_type=f32)
        .astype(bf16)
        .reshape(count_rows, heads_here, HD)
    )
    delta = jnp.sum(d_context.astype(f32) * context32.reshape(count_rows, heads_here, HD), -1)
    dctx_blocks = d_context.reshape(count_blocks, block, heads_here, HD)

    def backward_block(args):
        query_blk, block_index, block_seg, dctx_blk, delta_blk, lse_blk = args
        scores = masked_scores(query_blk, block_index, block_seg, all_keys, key_seg)
        probs = jnp.exp(scores - lse_blk[..., None]).astype(bf16)
        d_probs = jnp.einsum("qhe,khe->hqk", dctx_blk, all_values, preferred_element_type=f32)
        d_scores = (probs.astype(f32) * (d_probs - jnp.transpose(delta_blk)[..., None])).astype(
            bf16
        )
        d_query_blk = (
            jnp.einsum("hqk,khe->qhe", d_scores, all_keys, preferred_element_type=f32) * scale
        )
        return (probs, d_scores, d_query_blk)

    probs_all, dscores_all, d_queries = lax.map(
        backward_block,
        (
            query_blocks,
            index_blocks,
            seg_blocks,
            dctx_blocks,
            delta.reshape(count_blocks, block, heads_here),
            lse_all,
        ),
    )
    d_queries = d_queries.reshape(count_rows, heads_here, HD)
    key_part = (
        jnp.einsum("bhqk,bqhe->khe", dscores_all, query_blocks, preferred_element_type=f32) * scale
    )
    value_part = jnp.einsum("bhqk,bqhe->khe", probs_all, dctx_blocks, preferred_element_type=f32)
    key_value = lax.psum_scatter(
        jnp.concatenate(
            [
                key_part.reshape(count_rows * lax.axis_size("ctx"), local_width),
                value_part.reshape(count_rows * lax.axis_size("ctx"), local_width),
            ],
            axis=1,
        ),
        "ctx",
        scatter_dimension=0,
        tiled=True,
    )
    d_keys = key_value[:, :local_width].reshape(count_rows, heads_here, HD)
    d_values = key_value[:, local_width:]
    d_joint = jnp.stack(
        [
            unrotate(d_queries, cosine, sine).reshape(count_rows, local_width),
            unrotate(d_keys, cosine, sine).reshape(count_rows, local_width),
            d_values,
        ],
        axis=1,
    )
    d_joint_b = d_joint.astype(bf16)
    grad_joint_w = jnp.einsum("nd,npe->dpe", first, d_joint_b, preferred_element_type=f32)
    grad_joint_b = jnp.sum(d_joint, 0)
    d_first_part = jnp.einsum("npe,dpe->nd", d_joint_b, back_joint, preferred_element_type=f32)
    d_first, d_second = lax.psum((d_first_part, d_second_part), "tp")
    norm_stats = jnp.stack(
        [
            jnp.sum(d_first * normed, 0),
            jnp.sum(d_first, 0),
            jnp.sum(d_second * normed, 0),
            jnp.sum(d_second, 0),
        ]
    )
    tokens_grad = (
        cot
        + norm_back(d_first, normed, rstd, gain_one)
        + norm_back(d_second, normed, rstd, gain_two)
    )
    grad_small = jnp.concatenate([norm_stats, bias_sum[None], bias_sum[None]], axis=0)
    share_joint, share_output, share_up, share_down, share_small, share_jbias, share_upbias = (
        lax.psum_scatter(grad_joint_w, ("fsdp", "ctx"), scatter_dimension=0, tiled=True),
        lax.psum_scatter(grad_output_w, ("fsdp", "ctx"), scatter_dimension=1, tiled=True),
        lax.psum_scatter(grad_up_w, ("fsdp", "ctx"), scatter_dimension=0, tiled=True),
        lax.psum_scatter(grad_down_w, ("fsdp", "ctx"), scatter_dimension=1, tiled=True),
        lax.psum_scatter(grad_small, ("fsdp", "ctx"), scatter_dimension=1, tiled=True),
        lax.psum_scatter(grad_joint_b, ("fsdp", "ctx"), scatter_dimension=1, tiled=True),
        lax.psum_scatter(grad_up_b, ("fsdp", "ctx"), scatter_dimension=0, tiled=True),
    )
    owned = (
        lax.all_gather(share_joint, "ctx", axis=0, tiled=True),
        lax.all_gather(share_output, "ctx", axis=1, tiled=True),
        lax.all_gather(share_up, "ctx", axis=0, tiled=True),
        lax.all_gather(share_down, "ctx", axis=1, tiled=True),
        lax.all_gather(share_small, "ctx", axis=1, tiled=True),
        lax.all_gather(share_jbias, "ctx", axis=1, tiled=True),
        lax.all_gather(share_upbias, "ctx", axis=0, tiled=True),
    )
    owned_joint, owned_output, owned_up, owned_down, owned_small, owned_jbias, owned_upbias = owned
    return (
        result[None],
        tokens_grad[None],
        owned_small[0],
        owned_small[1],
        owned_small[2],
        owned_small[3],
        owned_joint,
        owned_jbias,
        owned_output,
        owned_small[4],
        owned_up,
        owned_upbias,
        owned_down,
        owned_small[5],
    )


NEG = -1e30


def attention_body(
    heads, flips, place_ref, *refs,
):
    f32 = jnp.float32
    bf16 = jnp.bfloat16
    ins, refs = refs[: 2 * flips], refs[2 * flips :]
    kseg_ref, qseg_ref, refs = refs[0], refs[1], refs[2:]
    outs, refs = refs[:flips], refs[flips:]
    x_ref, y_ref, kt_ref, vt_ref, s_ref, e_ref, dk_acc, dv_acc = refs
    step = pl.program_id(0)
    place = place_ref[0]
    rows = s_ref.shape[2]
    width = dk_acc.shape[1]
    chunks, _, chunk = kt_ref.shape
    hd = width // heads
    span = ins[0].shape[0]

    def spot(flip):
        return pl.ds(pl.multiple_of((place ^ flip) * span, span), span)

    k_ref = x_ref.at[:, width : 2 * width]
    v_ref = x_ref.at[:, 2 * width : 3 * width]

    @pl.when(step == 0)
    def _():
        for flip in range(flips):
            x_ref[spot(flip), : 3 * width] = ins[flip][...]
            x_ref[spot(flip), 3 * width :] = ins[flips + flip][...]
        for c in range(chunks):
            part = pl.ds(c * chunk, chunk)
            kt_ref[c] = k_ref[part, :].astype(f32).T.astype(bf16)
            vt_ref[c] = v_ref[part, :].astype(f32).T.astype(bf16)
        dk_acc[...] = jnp.zeros_like(dk_acc)
        dv_acc[...] = jnp.zeros_like(dv_acc)

    here = pl.ds(pl.multiple_of(step * rows, rows), rows)
    used = ((step + 1) * rows + chunk - 1) // chunk
    q = x_ref[here, :width]
    q_t = q.astype(f32).T
    dc_t = x_ref[here, 3 * width :].astype(f32).T
    row_head = lax.broadcasted_iota(jnp.int32, (width, rows), 0) // hd
    lane_head = lax.broadcasted_iota(jnp.int32, (rows, width), 1) // hd
    q_heads_t = [jnp.where(row_head == h, q_t, 0.0).astype(bf16) for h in range(heads)]
    q_heads = [jnp.where(lane_head == h, q, jnp.zeros_like(q)) for h in range(heads)]
    qseg = qseg_ref[...]
    query = step * rows + lax.broadcasted_iota(jnp.int32, (1, rows), 1)
    key_base = lax.broadcasted_iota(jnp.int32, (chunk, 1), 0)

    def score(j, tops):
        part = pl.ds(pl.multiple_of(j * chunk, chunk), chunk)
        keys = k_ref[part, :]
        allowed = (kseg_ref[part, :] == qseg) & (key_base + j * chunk <= query)
        out = []
        for h in range(heads):
            s = jnp.dot(keys, q_heads_t[h], preferred_element_type=f32)
            s = jnp.where(allowed, s, NEG)
            s_ref[h, part, :] = s
            out.append(jnp.maximum(tops[h], jnp.max(s, 0, keepdims=True)))
        return tuple(out)

    tops = lax.fori_loop(
        0, used, score, tuple(jnp.full((1, rows), NEG, f32) for _ in range(heads))
    )

    def mix(j, carry):
        part = pl.ds(pl.multiple_of(j * chunk, chunk), chunk)
        values_t = vt_ref[j]
        out = []
        for h in range(heads):
            total, acc = carry[h]
            e = jnp.exp(s_ref[h, part, :] - tops[h])
            total = total + jnp.sum(e, 0, keepdims=True)
            e = e.astype(bf16)
            e_ref[h, part, :] = e
            acc = acc + jnp.dot(
                values_t[h * hd : (h + 1) * hd, :], e, preferred_element_type=f32
            )
            out.append((total, acc))
        return tuple(out)

    mixed = lax.fori_loop(
        0,
        used,
        mix,
        tuple((jnp.zeros((1, rows), f32), jnp.zeros((hd, rows), f32)) for _ in range(heads)),
    )
    ctx_parts, dcn_parts, deltas = [], [], []
    for h in range(heads):
        total, acc = mixed[h]
        inv = 1.0 / total
        ctx_h = acc * inv
        dc_h = dc_t[h * hd : (h + 1) * hd, :]
        deltas.append(jnp.sum(ctx_h * dc_h, 0, keepdims=True) * inv)
        ctx_parts.append(ctx_h)
        dcn_parts.append(dc_h * inv)
    y_ref[here, :width] = jnp.concatenate(ctx_parts, 0).T.astype(bf16)
    dcn_t = jnp.concatenate(dcn_parts, 0)
    dcn = dcn_t.T
    dcn_heads_t = [jnp.where(row_head == h, dcn_t, 0.0).astype(bf16) for h in range(heads)]
    dcn_heads = [jnp.where(lane_head == h, dcn, 0.0).astype(bf16) for h in range(heads)]

    def back(j, carry):
        part = pl.ds(pl.multiple_of(j * chunk, chunk), chunk)
        values = v_ref[part, :]
        keys_t = kt_ref[j]
        dk = dk_acc[part, :]
        dv = dv_acc[part, :]
        out = []
        for h in range(heads):
            e = e_ref[h, part, :]
            dp = jnp.dot(values, dcn_heads_t[h], preferred_element_type=f32)
            ds = (e.astype(f32) * (dp - deltas[h])).astype(bf16)
            out.append(
                carry[h]
                + jnp.dot(keys_t[h * hd : (h + 1) * hd, :], ds, preferred_element_type=f32)
            )
            dk = dk + jnp.dot(ds, q_heads[h], preferred_element_type=f32)
            dv = dv + jnp.dot(e, dcn_heads[h], preferred_element_type=f32)
        dk_acc[part, :] = dk
        dv_acc[part, :] = dv
        return tuple(out)

    dq = lax.fori_loop(
        0, used, back, tuple(jnp.zeros((hd, rows), f32) for _ in range(heads))
    )
    y_ref[here, width : 2 * width] = (jnp.concatenate(dq, 0).T * HD ** (-0.5)).astype(bf16)

    @pl.when(step == pl.num_programs(0) - 1)
    def _():
        y_ref[:, 2 * width : 3 * width] = dk_acc[...].astype(bf16)
        y_ref[:, 3 * width :] = dv_acc[...].astype(bf16)
        for flip in range(flips):
            outs[flip][...] = y_ref[spot(flip), :]


def attention(blocks, seg, place, block=256, chunk=256):
    flips = len(blocks) // 2
    span, width = blocks[-1].shape
    count, columns = span * flips, 4 * width
    heads = width // HD
    bf16 = jnp.bfloat16
    f32 = jnp.float32
    pairs = count * (count + block) // 2 * heads
    whole = pl.BlockSpec((span, columns), lambda i, p: (0, 0))
    return pl.pallas_call(
        lambda *refs: attention_body(heads, flips, *refs),
        grid_spec=pltpu.PrefetchScalarGridSpec(
            num_scalar_prefetch=1,
            grid=(count // block,),
            in_specs=[pl.BlockSpec(block.shape, lambda i, p: (0, 0)) for block in blocks]
            + [
                pl.BlockSpec((count, 1), lambda i, p: (0, 0)),
                pl.BlockSpec((1, block), lambda i, p: (0, i)),
            ],
            out_specs=[whole] * flips,
            scratch_shapes=[
                pltpu.VMEM((count, columns), bf16),
                pltpu.VMEM((count, columns), bf16),
                pltpu.VMEM((count // chunk, width, chunk), bf16),
                pltpu.VMEM((count // chunk, width, chunk), bf16),
                pltpu.VMEM((heads, count, block), f32),
                pltpu.VMEM((heads, count, block), bf16),
                pltpu.VMEM((count, width), f32),
                pltpu.VMEM((count, width), f32),
            ],
        ),
        out_shape=[jax.ShapeDtypeStruct((span, columns), bf16)] * flips,
        compiler_params=pltpu.CompilerParams(vmem_limit_bytes=48 * 1024 * 1024),
        cost_estimate=pl.CostEstimate(
            flops=10 * pairs * HD * 3, bytes_accessed=count * width * 16, transcendentals=pairs
        ),
        name="attention",
    )(place.reshape(1), *blocks, seg[:, None], seg[None, :])


def norm_rows(x, slot, params_ref, outs):
    bf16 = jnp.bfloat16
    first_ref, second_ref, normed_ref = outs
    normed, _ = normalize(x.astype(jnp.float32))
    normed_ref[0, slot] = normed.astype(bf16)
    first_ref[0, slot] = (normed * params_ref[0:1] + params_ref[1:2]).astype(bf16)
    second_ref[0, slot] = (normed * params_ref[2:3] + params_ref[3:4]).astype(bf16)


def merge_rows(x, slot, params_ref, outs):
    outs[0][0, slot] = x


def both_cores(rows_body, own, mine, other, core, params, results):
    size = len(mine) + 1
    half, cols = mine[0].shape

    def run(core_ref, *refs):
        own_ref, refs = refs[0], refs[1:]
        ins, params_ref, outs = refs[: 2 * size - 2], refs[2 * size - 2], refs[2 * size - 1 :]
        core = core_ref[0]

        @pl.when(pl.program_id(0) == 0)
        def _():
            for slot in range(2):
                rows_body(own_ref[slot * half : (slot + 1) * half, :], slot, params_ref, outs)

        for chip in range(1, size):

            @pl.when(pl.program_id(0) == chip)
            def _(chip=chip):
                rows_body(ins[chip - 1][...], core, params_ref, outs)
                rows_body(ins[size + chip - 2][...], 1 - core, params_ref, outs)

    made = pl.pallas_call(
        run,
        grid_spec=pltpu.PrefetchScalarGridSpec(
            num_scalar_prefetch=1,
            grid=(size,),
            in_specs=[pl.BlockSpec(own.shape, lambda i, c: (0, 0))]
            + [pl.BlockSpec((half, cols), lambda i, c: (0, 0))] * (2 * size - 2)
            + [pl.BlockSpec(params.shape, lambda i, c: (0, 0))],
            out_specs=[pl.BlockSpec((1, 2, half, cols), lambda i, c: (i, 0, 0, 0))] * results,
        ),
        out_shape=[jax.ShapeDtypeStruct((size, 2, half, cols), own.dtype)] * results,
        compiler_params=pltpu.CompilerParams(vmem_limit_bytes=32 * 1024 * 1024),
        cost_estimate=pl.CostEstimate(
            flops=size * half * cols * 20,
            bytes_accessed=size * half * cols * 4 * (1 + results),
            transcendentals=0,
        ),
        name=rows_body.__name__,
    )(core.reshape(1), own, *mine, *other, params)
    return [x.reshape(size * 2 * half, cols) for x in made]


def partner(tensor, axis, flip):
    size = lax.axis_size(axis)
    return lax.ppermute(tensor, axis, [(s, s ^ flip) for s in range(size)])


def pick(tensor, index, size, dim=0):
    return lax.dynamic_slice_in_dim(tensor, index * size, size, dim)


def swap(tensor, axis):
    return lax.all_to_all(tensor, axis, 0, 0)


def gather(block, axis):
    return swap(jnp.broadcast_to(block[None], (lax.axis_size(axis),) + block.shape), axis)


def chip_start(partial, size):
    f32 = jnp.float32
    core = lax.axis_index("tp")
    halves = partial.reshape(size, 2, -1, partial.shape[1])
    away = lax.dynamic_index_in_dim(halves, 1 - core, 1, keepdims=False)
    kept = lax.dynamic_index_in_dim(halves, core, 1, keepdims=False)
    return (kept.astype(f32) + partner(away, "tp", 1).astype(f32)).astype(partial.dtype)


def chip_join(mine, other):
    core = lax.axis_index("tp")
    low = jnp.where(core == 0, mine, other)
    high = jnp.where(core == 0, other, mine)
    return jnp.concatenate([low, high], 0)


def pack_wide(up, down, out, chips, part):
    span = down.shape[2] // chips
    for chip in range(chips):
        out[0, chip, :part, :] = up[chip, 0]
        for half in range(2):
            out[0, chip, part:, half * span : (half + 1) * span] = down[
                0, half * part : (half + 1) * part, chip * span : (chip + 1) * span
            ]


def pack_heads(joint, outw, out, low, chips, part):
    width = joint.shape[4]
    span = outw.shape[3] // chips // 2
    rows = part // 2
    for chip in range(chips):
        out[0, chip, :, :width] = joint[chip, 0, low]
        for half in range(2):
            begin = (2 * chip + half) * span
            out[0, chip, half * rows : (half + 1) * rows, width:] = outw[
                0, low, :, begin : begin + span
            ]


def unpack_wide(x, up, down, chips, part):
    f32 = jnp.float32
    span = down.shape[3]
    cols = x.shape[2]
    for chip in range(chips):
        up[:, chip * cols : (chip + 1) * cols] = x[chip, :part, :].astype(f32)
        for half in range(2):
            down[chip, 0, half * part : (half + 1) * part, :] = x[
                chip, part:, half * span : (half + 1) * span
            ].astype(f32)


def unpack_heads(x, joint, outw, chips, part):
    f32 = jnp.float32
    span = outw.shape[3] // 2
    rows = part // 2
    width = joint.shape[2] // chips
    for chip in range(chips):
        for kind in range(3):
            joint[kind, :, chip * width : (chip + 1) * width] = x[
                chip, :, kind * width : (kind + 1) * width
            ].astype(f32)
        for half in range(2):
            outw[chip, 0, :, half * span : (half + 1) * span] = x[
                chip, half * rows : (half + 1) * rows, 3 * width :
            ].astype(f32)


def unpack(body, blocks, wide, wide_block, tall, tall_block, place):
    f32 = jnp.float32
    chips, rows, cols = blocks[0].shape
    depth = len(blocks)
    whole = pl.BlockSpec((chips, rows, cols), lambda i, p: (0, 0, 0))

    def run(place_ref, *refs):
        for k in range(depth):

            @pl.when(pl.program_id(0) == k)
            def _(k=k):
                body(refs[k], refs[depth], refs[depth + 1], chips, cols // 8)

    def at(dim, count):
        return lambda i, p: tuple((p[0] ^ i) if d == dim else 0 for d in range(count))

    dim = len(wide) - 2
    return pl.pallas_call(
        run,
        grid_spec=pltpu.PrefetchScalarGridSpec(
            num_scalar_prefetch=1,
            grid=(depth,),
            in_specs=[whole] * depth,
            out_specs=[
                pl.BlockSpec(wide_block, at(dim, len(wide))),
                pl.BlockSpec(tall_block, at(1, len(tall))),
            ],
        ),
        out_shape=[jax.ShapeDtypeStruct(wide, f32), jax.ShapeDtypeStruct(tall, f32)],
        compiler_params=pltpu.CompilerParams(vmem_limit_bytes=24 * 1024 * 1024),
        cost_estimate=pl.CostEstimate(
            flops=0, bytes_accessed=6 * depth * chips * rows * cols, transcendentals=0
        ),
        name=body.__name__,
    )(place.reshape(1), *blocks)


def pack_slots(body, wide, tall, rows, chips, place):
    depth = 4
    part = wide.shape[0] // chips // depth
    cols = part * 8
    wide = wide.reshape(chips, 1, depth, part, wide.shape[1])
    tall = tall.reshape(1, depth, tall.shape[0] // depth, tall.shape[1])

    def run(place_ref, wide_ref, tall_ref, *outs):
        for k in range(depth):
            body(wide_ref, tall_ref, outs[k], place_ref[0] ^ k, chips, part)

    return pl.pallas_call(
        run,
        grid_spec=pltpu.PrefetchScalarGridSpec(
            num_scalar_prefetch=1,
            grid=(1,),
            in_specs=[
                pl.BlockSpec(wide.shape, lambda i, p: (0, 0, 0, 0, 0)),
                pl.BlockSpec(tall.shape, lambda i, p: (0, 0, 0, 0)),
            ],
            out_specs=[pl.BlockSpec((1, chips, rows, cols), lambda i, p: (0, 0, 0, 0))] * depth,
        ),
        out_shape=[jax.ShapeDtypeStruct((1, chips, rows, cols), jnp.bfloat16)] * depth,
        compiler_params=pltpu.CompilerParams(vmem_limit_bytes=24 * 1024 * 1024),
        cost_estimate=pl.CostEstimate(
            flops=0, bytes_accessed=16 * chips * rows * cols, transcendentals=0
        ),
        name=body.__name__,
    )(place.reshape(1), wide, tall)


def pack_all(body, wide, tall, rows, chips):
    depth = 4
    part = wide.shape[0] // chips // depth
    cols = part * 8
    wide = wide.reshape(chips, depth, part, wide.shape[1])
    tall = tall.reshape(depth, tall.shape[0] // depth, tall.shape[1])

    def run(wide_ref, tall_ref, out):
        body(wide_ref, tall_ref, out, chips, part)

    return pl.pallas_call(
        run,
        grid=(depth,),
        in_specs=[
            pl.BlockSpec((chips, 1, part, wide.shape[3]), lambda i: (0, i, 0, 0)),
            pl.BlockSpec((1,) + tall.shape[1:], lambda i: (i, 0, 0)),
        ],
        out_specs=pl.BlockSpec((1, chips, rows, cols), lambda i: (i, 0, 0, 0)),
        out_shape=jax.ShapeDtypeStruct((depth, chips, rows, cols), jnp.bfloat16),
        compiler_params=pltpu.CompilerParams(vmem_limit_bytes=24 * 1024 * 1024),
        cost_estimate=pl.CostEstimate(
            flops=0, bytes_accessed=4 * depth * chips * rows * cols, transcendentals=0
        ),
        name="pack_wide",
    )(wide, tall)


def add_slots(slots):
    total = slots[0][0].astype(jnp.float32)
    for slot in slots[1:]:
        total = total + slot[0].astype(jnp.float32)
    return total.astype(jnp.bfloat16)


def send_slots(slots):
    return [slots[0]] + [partner(slots[k], "ctx", k) for k in range(1, len(slots))]


def after(tensor, *others):
    return lax.optimization_barrier((tensor,) + others)[0]


def hidden_body(second_ref, cot_ref, up_ref, down_ref, bias_ref, act_ref, dup_ref, sum_ref):
    f32 = jnp.float32
    bf16 = jnp.bfloat16
    upper = jnp.dot(second_ref[...], up_ref[...], preferred_element_type=f32)
    upper = upper + bias_ref[...]
    share = 0.5 + 0.5 * lax.erf(upper * 0.5**0.5)
    act_ref[...] = (upper * share).astype(bf16)
    d_act = lax.dot_general(
        cot_ref[...], down_ref[...], (((1,), (1,)), ((), ())), preferred_element_type=f32
    )
    bell = jnp.exp(-0.5 * upper * upper) * (0.5 / jnp.pi) ** 0.5
    d_upper = d_act * (share + upper * bell)
    dup_ref[...] = d_upper.astype(bf16)

    @pl.when(pl.program_id(0) == 0)
    def _():
        sum_ref[...] = jnp.zeros_like(sum_ref)

    sum_ref[...] += jnp.sum(d_upper, 0, keepdims=True)


def hidden_layer(second, cot_b, up_w, down_w, up_bias, block=256):
    f32 = jnp.float32
    bf16 = jnp.bfloat16
    count, model = second.shape
    hidden = up_w.shape[1]
    rows = pl.BlockSpec((block, model), lambda i: (i, 0))
    made = pl.BlockSpec((block, hidden), lambda i: (i, 0))
    act, dup, total = pl.pallas_call(
        hidden_body,
        grid=(count // block,),
        in_specs=[
            rows,
            rows,
            pl.BlockSpec((model, hidden), lambda i: (0, 0)),
            pl.BlockSpec((hidden, model), lambda i: (0, 0)),
            pl.BlockSpec((1, hidden), lambda i: (0, 0)),
        ],
        out_specs=[made, made, pl.BlockSpec((1, hidden), lambda i: (0, 0))],
        out_shape=[
            jax.ShapeDtypeStruct((count, hidden), bf16),
            jax.ShapeDtypeStruct((count, hidden), bf16),
            jax.ShapeDtypeStruct((1, hidden), f32),
        ],
        compiler_params=pltpu.CompilerParams(vmem_limit_bytes=32 * 1024 * 1024),
        cost_estimate=pl.CostEstimate(
            flops=4 * count * model * hidden,
            bytes_accessed=4 * count * (model + hidden) + 4 * model * hidden,
            transcendentals=2 * count * hidden,
        ),
        name="hidden_layer",
    )(second, cot_b, up_w, down_w, up_bias.astype(f32)[None])
    return act, dup, total[0]


def plane_local(
    tokens,
    segment_ids,
    positions,
    attention_gain,
    attention_shift,
    feedforward_gain,
    feedforward_shift,
    joint_weight,
    joint_bias,
    output_weight,
    output_bias,
    up_weight,
    up_bias,
    down_weight,
    down_bias,
    cotangent,
):
    f32 = jnp.float32
    bf16 = jnp.bfloat16
    me, place, core = lax.axis_index("fsdp"), lax.axis_index("ctx"), lax.axis_index("tp")
    size = lax.axis_size("fsdp")
    depth = lax.axis_size("ctx")
    count, model = tokens.shape[1:]
    half_rows = count // 2
    rows = tokens[0].astype(f32)
    cot = cotangent[0]

    half = pick(tokens[0], core, half_rows)
    my_tokens = [partner(half, "fsdp", k) for k in range(1, size)]
    cot_half, _ = lax.optimization_barrier((cot.astype(bf16), tuple(my_tokens)))
    half = pick(cot_half, core, half_rows)
    my_cot = [partner(half, "fsdp", k) for k in range(1, size)]
    width = joint_weight.shape[2] // size
    small = jnp.concatenate(
        [
            attention_gain,
            attention_shift,
            feedforward_gain,
            feedforward_shift,
            output_bias,
            down_bias,
        ]
    ).astype(f32)
    notes = jnp.concatenate([small, segment_ids[0].astype(f32), positions[0].astype(f32)])
    packed = gather(
        notes,
        ("fsdp", "ctx"),
    ).reshape(size, depth, -1)
    joint_send = joint_weight.reshape(-1, 3, size, width).transpose(2, 0, 1, 3)
    tokens_other = [partner(block, "tp", 1) for block in my_tokens]
    joint_w = swap(after(joint_send, packed), "fsdp")
    joint_w = after(joint_w, *tokens_other).reshape(model, 3, width)
    params = packed[:, 0, : small.size].reshape(size, 6, -1).transpose(1, 0, 2).reshape(6, model)
    seg_seq = lax.dynamic_index_in_dim(packed, place, 0, keepdims=False)
    seg_seq = seg_seq[:, small.size : small.size + count].reshape(-1)
    pos_here = lax.dynamic_index_in_dim(packed, place, 1, keepdims=False)[:, small.size + count :]
    pos_plane = jnp.concatenate(
        [lax.dynamic_index_in_dim(pos_here, me ^ k, 0, keepdims=False) for k in range(size)]
    )
    first, second, normed = both_cores(
        norm_rows, tokens[0], my_tokens, tokens_other, core, params[:4], 3
    )
    output_w = swap(after(output_weight, first).reshape(size, width, -1), "fsdp")
    output_w = output_w.transpose(1, 0, 2).reshape(width, model)
    cot_other = [partner(block, "tp", 1) for block in my_cot]
    (cot_b,) = both_cores(merge_rows, cot_half, my_cot, cot_other, core, params[:4], 1)
    hidden = up_weight.shape[1] // size
    up_send = up_weight.reshape(-1, size, hidden).transpose(1, 0, 2)
    up_w = swap(after(up_send, output_w, first, cot_b), "fsdp")
    up_w = up_w.reshape(model, hidden)


    lane = jnp.arange(width, dtype=jnp.int32) % HD
    half = ROT // 2
    freq = jnp.where(
        lane < ROT, ROPE_BASE ** (-((lane % half).astype(f32) * 2.0 / ROT)), 0.0
    )
    angle = pos_plane[:, None] * freq[None, :]
    cosine = jnp.cos(angle)
    sine = jnp.sin(angle) * jnp.where(lane < half, -1.0, 1.0)[None, :]
    source = jnp.arange(width, dtype=jnp.int32)
    source = jnp.where(lane < half, source + half, jnp.where(lane < ROT, source - half, -1))
    turn = (jnp.arange(width, dtype=jnp.int32)[:, None] == source[None, :]).astype(bf16)

    joint_flat = joint_w.reshape(model, 3 * width)
    bias = joint_bias.astype(f32)
    joint = jnp.dot(first, joint_flat, preferred_element_type=f32) + bias.reshape(-1)[None]
    swapped_w = jnp.einsum("dpe,ef->dpf", joint_w[:, :2], turn, preferred_element_type=bf16)
    swapped_b = jnp.dot(joint_bias[:2], turn, preferred_element_type=f32)
    swapped = (
        jnp.dot(first, swapped_w.reshape(model, 2 * width), preferred_element_type=f32)
        + swapped_b.reshape(-1)[None]
    )
    scale = HD ** (-0.5)
    queries = (joint[:, :width] * cosine + swapped[:, :width] * sine) * scale
    keys = joint[:, width : 2 * width] * cosine + swapped[:, width:] * sine
    d_context = jnp.einsum("nd,wd->nw", cot_b, output_w, preferred_element_type=f32)
    sending = jnp.concatenate([queries, keys, joint[:, 2 * width :]], 1).astype(bf16)
    blocks = []
    for tensor in (sending, d_context.astype(bf16)):
        for flip in range(depth):
            block = pick(tensor, me ^ place ^ flip, count)
            blocks.append(partner(block, "ctx", flip) if flip else block)
    down_w = swap(after(down_weight, up_w, blocks[2]).reshape(size, hidden, -1), "fsdp")
    down_w = down_w.transpose(1, 0, 2).reshape(hidden, model)
    second, up_w = lax.optimization_barrier((second, up_w, sending))[:2]

    activated, d_upper_b, grad_up_b = hidden_layer(second, cot_b, up_w, down_w, up_bias)
    moment_up = jnp.dot(normed.T, d_upper_b, preferred_element_type=f32)
    d_upper_sum = jnp.sum(d_upper_b.astype(f32), 0)
    grad_up_w = (
        params[2][:, None] * moment_up + params[3][:, None] * d_upper_sum[None, :]
    ).astype(bf16)
    up_f32 = up_w.astype(f32)
    gain_two_grad = jnp.sum(up_f32 * moment_up, 1)
    shift_two_grad = jnp.sum(up_f32 * d_upper_sum[None, :], 1)
    grad_down_w = jnp.dot(activated.T, cot_b, preferred_element_type=f32).astype(bf16)
    part = model // size // depth
    packed_wide = pack_all(pack_wide, grad_up_w, grad_down_w, 2 * part, size)
    blocks, packed_wide = lax.optimization_barrier((tuple(blocks), packed_wide))
    made = attention(blocks, seg_seq, place)
    made, packed_wide = lax.optimization_barrier((tuple(made), swap(packed_wide, "ctx")))
    held_wide = swap(jnp.sum(packed_wide.astype(f32), 0).astype(bf16), "fsdp")
    gained = (up_f32 * params[2][:, None]).astype(bf16)
    upstream_two = jnp.einsum("nf,df->nd", d_upper_b, gained, preferred_element_type=f32)
    upstream_two = upstream_two.astype(bf16)
    mixed_two = jnp.dot(activated, down_w, preferred_element_type=f32).astype(bf16)

    back = jnp.zeros((size * count, 4 * width), bf16)
    made = [made[0]] + [partner(made[k], "ctx", k) for k in range(1, depth)]
    made, held_wide = lax.optimization_barrier((tuple(made), held_wide))
    near_far = partner(held_wide, "ctx", 1), partner(held_wide, "ctx", 2)
    for flip in range(depth):
        block = made[flip]
        back = lax.dynamic_update_slice_in_dim(back, block, (me ^ place ^ flip) * count, 0)
    context = back[:, :width]
    d_qk = back[:, width : 3 * width]

    d_swapped = jnp.einsum(
        "npe,ef->npf", d_qk.reshape(-1, 2, width), turn, preferred_element_type=f32
    ).reshape(-1, 2 * width)
    cosines = jnp.concatenate([cosine, cosine], 1)
    sines = jnp.concatenate([sine, sine], 1)
    d_joint = jnp.concatenate(
        [d_qk.astype(f32) * cosines - d_swapped * sines, back[:, 3 * width :].astype(f32)], 1
    )
    d_joint_b = d_joint.astype(bf16)
    joint_f32 = joint_flat.astype(f32)
    gained = (joint_f32 * params[0][:, None]).astype(bf16)
    mixed = jnp.dot(context, output_w, preferred_element_type=f32) + mixed_two.astype(f32)
    mixed = mixed.astype(bf16)
    upstream = jnp.einsum("ne,de->nd", d_joint_b, gained, preferred_element_type=f32)
    upstream = (upstream + upstream_two.astype(f32)).astype(bf16)
    d_joint_b, context = lax.optimization_barrier((d_joint_b, context, mixed, upstream))[:2]
    sending_result = chip_start(mixed, size)
    sending_up = chip_start(upstream, size)
    got_result = partner(sending_result[2:], "fsdp", 2)
    got_up = partner(sending_up[1::2], "fsdp", 1)
    grad_joint_b = jnp.sum(d_joint, 0)
    moment_joint = jnp.dot(normed.T, d_joint_b, preferred_element_type=f32)
    d_joint_sum = jnp.sum(d_joint_b.astype(f32), 0)
    grad_joint_w = (
        params[0][:, None] * moment_joint + params[1][:, None] * d_joint_sum[None, :]
    ).astype(bf16)
    grad_output_w = jnp.dot(context.T, cot_b, preferred_element_type=f32).astype(bf16)
    slots = pack_slots(pack_heads, grad_joint_w, grad_output_w, part, size, place)
    slots = send_slots(slots)
    stats = jnp.stack(
        [
            jnp.sum(joint_f32 * moment_joint, 1),
            jnp.sum(joint_f32 * d_joint_sum[None, :], 1),
            gain_two_grad,
            shift_two_grad,
            jnp.sum(pick(cot, core, half_rows), 0),
        ]
    )
    stats = stats.reshape(5, size, 1, -1).transpose(1, 2, 0, 3).reshape(size, 1, -1)
    biases = jnp.concatenate([grad_joint_b, grad_up_b])
    biases = jnp.broadcast_to(biases[None, None], (size, 1, 3 * width + hidden))
    stats_size = stats.shape[2]
    packed = jnp.concatenate([stats, biases], 2)
    packed = jnp.broadcast_to(packed, (size, 2 * depth, packed.shape[2]))
    packed = swap(packed.reshape(2 * size * depth, 1, -1), ("fsdp", "ctx", "tp"))
    got_result, got_up = lax.optimization_barrier((got_result, got_up))
    half_result = sending_result[:2].astype(f32) + got_result.astype(f32)
    half_up = sending_up[::2].astype(f32) + got_up.astype(f32)
    got_result = partner(half_result[1].astype(bf16), "fsdp", 1)
    got_up = partner(half_up[1].astype(bf16), "fsdp", 2)
    slots, near_far, got_result, got_up, packed = lax.optimization_barrier(
        (tuple(slots), near_far, got_result, got_up, packed)
    )

    held = swap(add_slots(slots), "fsdp")
    last = partner(near_far[1], "ctx", 1)
    my_rows = pick(rows, core, half_rows)
    result = my_rows + half_result[0] + got_result.astype(f32) + params[4] + params[5]
    normed_here, rstd = normalize(my_rows)
    upstream = half_up[0] + got_up.astype(f32)
    tokens_grad = pick(cot, core, half_rows) + rstd * (
        upstream
        - jnp.mean(upstream, -1, keepdims=True)
        - normed_here * jnp.mean(upstream * normed_here, -1, keepdims=True)
    )
    other_result = partner(result, "tp", 1)
    other_grad = partner(tokens_grad, "tp", 1)
    held, last, other_result, other_grad = lax.optimization_barrier(
        (held, last, other_result, other_grad)
    )

    slots = send_slots([held[None]] * depth)
    result = chip_join(result, other_result)
    tokens_grad = chip_join(tokens_grad, other_grad)
    packed = packed.reshape(size, depth, 2, -1)
    owned = jnp.sum(packed[..., :stats_size], (0, 1, 2)).reshape(5, -1)
    biases = lax.dynamic_index_in_dim(packed[..., stats_size:], me, 0, keepdims=False)
    biases = jnp.sum(lax.dynamic_index_in_dim(biases, core, 1, keepdims=False), 0)
    owned_jbias = biases[: 3 * width].reshape(3, width)
    owned_upbias = biases[3 * width :]
    owned_up, owned_down = unpack(
        unpack_wide,
        (held_wide, near_far[0], near_far[1], last),
        (model // size, up_weight.shape[1]),
        (part, up_weight.shape[1]),
        (size, depth, 2 * part, 2 * width),
        (size, 1, 2 * part, 2 * width),
        place,
    )
    owned_down = owned_down.reshape(down_weight.shape)
    owned_joint, owned_output = unpack(
        unpack_heads,
        [slot[0] for slot in slots],
        (3, model // size, joint_weight.shape[2]),
        (3, part, joint_weight.shape[2]),
        (size, depth, part // 2, 2 * width),
        (size, 1, part // 2, 2 * width),
        place,
    )
    owned_joint = owned_joint.transpose(1, 0, 2)
    owned_output = owned_output.reshape(output_weight.shape)
    return (
        result[None],
        tokens_grad[None],
        owned[0],
        owned[1],
        owned[2],
        owned[3],
        owned_joint,
        owned_jbias,
        owned_output,
        owned[4],
        owned_up,
        owned_upbias,
        owned_down,
        owned[4],
    )


def splits_plane(mesh, tokens, joint_weight, up_weight):
    size, depth, cores = mesh.shape["fsdp"], mesh.shape["ctx"], mesh.shape["tp"]
    width = joint_weight.shape[2] // (size * cores)
    return (
        size == depth == tokens.shape[0] == 4
        and cores == 2
        and width % 128 == 0
        and tokens.shape[2] == 2 * size * width
        and up_weight.shape[1] == 4 * size * cores * width
        and tokens.shape[1] // depth % 256 == 0
    )


def solution(mesh):
    placed = (
        P("fsdp", "ctx", None),
        P("fsdp", "ctx"),
        P("fsdp", "ctx"),
        P("fsdp"),
        P("fsdp"),
        P("fsdp"),
        P("fsdp"),
        P("fsdp", None, "tp"),
        P(None, ("tp", "fsdp")),
        P("tp", "fsdp"),
        P("fsdp"),
        P("fsdp", "tp"),
        P(("tp", "fsdp")),
        P("tp", "fsdp"),
        P("fsdp"),
        P("fsdp", "ctx", None),
    )
    given = (
        P("fsdp", "ctx", None),
        P("fsdp", "ctx", None),
        P("fsdp"),
        P("fsdp"),
        P("fsdp"),
        P("fsdp"),
        P("fsdp", None, "tp"),
        P(None, ("tp", "fsdp")),
        P("tp", "fsdp"),
        P("fsdp"),
        P("fsdp", "tp"),
        P(("tp", "fsdp")),
        P("tp", "fsdp"),
        P("fsdp"),
    )

    def run(*args):
        body = plane_local if splits_plane(mesh, args[0], args[7], args[11]) else gathered_local
        return jax.shard_map(
            body, mesh=mesh, in_specs=placed, out_specs=given, check_vma=False
        )(*args)

    return run
```
